32 devices in a mesh: ctx: 8 (over y, x, core), exp: 4 (over z).
Axes of the slice: x: 2, y: 2, z: 4, core: 2. Of those that a mesh axis runs over, the one named last changes fastest.
Arguments:
- tokens: bfloat16 [4096, 2048], P(('ctx', 'exp')), may hold values from -6 to 6
- cotangent: bfloat16 [4096, 2048], P(('ctx', 'exp')), may hold values from -6 to 6
- expert_ids: int32 [4096, 1], P(('ctx', 'exp')), may hold values from 0 to 3; in each aligned block of 128 rows (0 to 127, 128 to 255, ...) at most 48 rows name the same one
- route_weights: float32 [4096, 1], P(('ctx', 'exp')), may hold values from 0.1 to 1
- w_gate: bfloat16 [4, 2048, 768], P('exp', 'ctx'), may hold values from -0.125 to 0.125
- w_up: bfloat16 [4, 2048, 768], P('exp', 'ctx'), may hold values from -0.125 to 0.125
- w_down: bfloat16 [4, 768, 2048], P('exp', None, 'ctx'), may hold values from -0.21875 to 0.21875
Outputs:
- token_grads: bfloat16 [4096, 2048], P(('ctx', 'exp'))
- route_grads: float32 [4096, 1], P(('ctx', 'exp'))
- gate_grads: bfloat16 [4, 2048, 768], P('exp', 'ctx')
- up_grads: bfloat16 [4, 2048, 768], P('exp', 'ctx')
- down_grads: bfloat16 [4, 768, 2048], P('exp', None, 'ctx')
The draws below stay inside these ranges and needn't reach their ends.
Inputs may be any that keep to these rules, and one draw needn't show every extreme that they name: `expert_ids`: among the 128 routes of one device's tokens no expert is named more than 48 times, a bound that some block reaches; the routes of one token name different experts.
All inputs are finite; a program needn't handle non-finite values.
Results may differ from the reference program's by a relative error of at most 0.018.
Values may be sent and summed in bfloat16 or wider, within the bound.
A program may use at most 64 MiB of HBM per device.

```python
import math
import jax
import jax.numpy as jnp
import numpy as np
from jax import lax

D = 2048
FF = 768
TOK_DEV = 128
ROUTES = 1
EXPERTS = 4
CAP = 48
TOKENS = 4096
N_CTX = 8
N_EXP = 4


def levels(own_key, shape, split, low, high):
    def one(axis_at, blocks):
        heights = jax.random.uniform(jax.random.fold_in(jax.random.fold_in(own_key, 6), axis_at), (blocks,), jnp.float32, low / len(split), high / len(split))
        return jnp.repeat(jnp.exp(heights), shape[axis_at] // blocks).reshape((-1,) + (1,) * (len(shape) - axis_at - 1))

    loudness = one(*split[0])
    for cut in split[1:]:
        loudness = loudness * one(*cut)
    return loudness


def routed_block(own_key, own, number, rows, number_of, top, reach, slope):
    sequence = jax.random.permutation(own_key, number_of)
    crowded, ordinary = portions_of(number_of, rows * top, reach, slope, True), portions_of(number_of, rows * top, reach, slope, False)
    places = jnp.arange(number_of)

    def named(sizes, turn):
        used = int((sizes > 0).sum())
        fixed = max(1, used // 4)
        moved = fixed + (places - fixed + turn * (used - fixed)) % max(1, number_of - fixed)
        return jnp.zeros((number_of,), jnp.int32).at[sequence[jnp.where(places < fixed, places, moved)]].set(jnp.asarray(sizes, jnp.int32))

    sizes = jnp.where(number % 4 == 0, named(crowded, number // 4), named(ordinary, number - number // 4 - 1))
    mixed = jax.random.permutation(jax.random.fold_in(own, 3), number_of)
    donor, receiver = mixed[0:number_of // 2 * 2:2], mixed[1:number_of // 2 * 2:2]
    slack = jnp.minimum(sizes[donor] - 1, reach - sizes[receiver]) // 2
    slack = jnp.where((donor == sequence[0]) | (receiver == sequence[0]) | (sizes[receiver] == 0), 0, jnp.maximum(slack, 0))
    moved = jax.random.randint(jax.random.fold_in(own, 4), (number_of // 2,), 0, 1 << 20) % (slack + 1)
    sizes = sizes.at[donor].add(-moved).at[receiver].add(moved)
    items = jnp.searchsorted(jnp.cumsum(sizes), jnp.arange(rows * top), side="right").astype(jnp.int32)
    grid = items.reshape(top, rows).T
    grid = grid[jax.random.permutation(jax.random.fold_in(own, 1), rows)]
    turn = jax.random.randint(jax.random.fold_in(own, 2), (rows, 1), 0, top)
    return jnp.take_along_axis(grid, (jnp.arange(top)[None, :] + turn) % top, axis=1)


def portions_of(count, total, bound, slope, full):
    portions = [(1 << 20) // math.isqrt(rank ** slope) + 1 for rank in range(1, count + 1)]
    largest = bound if full else min(bound, max(-(-total // count), total * portions[0] // sum(portions)))
    least = 1 if total - largest >= count - 1 else 0
    given, rest = [largest] + [least] * (count - 1), total - largest - least * (count - 1)
    while rest > 0:
        movable = [i for i in range(1, count) if given[i] < largest] or [i for i in range(1, count) if given[i] < bound]
        whole, budget = sum([portions[i] for i in movable]), rest
        for i in movable:
            addition = min(bound - given[i], max(1, budget * portions[i] // whole), rest)
            given[i] = given[i] + addition
            rest = rest - addition
    return np.array(given)


def gaussian(rng, extent, deviation, limit, shards=(), held_as=jnp.bfloat16):
    drawn = jax.random.normal(rng, extent, jnp.float32) * deviation
    if len(shards) > 0:
        drawn = levels(rng, extent, shards, -0.22, 0.18) * drawn
    return jnp.clip(drawn, min=-limit, max=limit).astype(held_as)


def setup_inputs(seed: int = 0) -> dict:
    streams_of = jax.random.split(jax.random.key(seed), 8)
    tokens = gaussian(streams_of[0], (TOKENS, D), 1.0, 6.0, ((0, 32),))
    cotangent = gaussian(streams_of[1], (TOKENS, D), 1.0, 6.0, ((0, 32),))
    expert_ids_keys = jax.random.split(jax.random.fold_in(streams_of[2], 1), TOKENS // TOK_DEV)
    expert_ids_turns = jax.random.permutation(jax.random.fold_in(streams_of[2], 3), TOKENS // TOK_DEV)
    expert_ids = jax.vmap(lambda own, number: routed_block(jax.random.fold_in(streams_of[2], 2), own, number, TOK_DEV, EXPERTS, ROUTES, CAP, 2))(expert_ids_keys, expert_ids_turns).reshape((TOKENS, ROUTES))
    route_weights = jnp.clip(jnp.exp(math.log(1.0) - 2.3025851 * jax.random.uniform(streams_of[3], (TOKENS, ROUTES), jnp.float32) ** levels(streams_of[3], (TOKENS, ROUTES), ((0, 32),), -0.2, 0.2)), 0.1, 1.0)
    w_gate = gaussian(streams_of[4], (EXPERTS, D, FF), D ** -0.5, 0.125, ((0, 4), (1, 8)))
    w_up = gaussian(streams_of[5], (EXPERTS, D, FF), D ** -0.5, 0.125, ((0, 4), (1, 8)))
    w_down = gaussian(streams_of[6], (EXPERTS, FF, D), FF ** -0.5, 0.21875, ((0, 4), (2, 8)))
    return dict(tokens=tokens, cotangent=cotangent, expert_ids=expert_ids, route_weights=route_weights, w_gate=w_gate, w_up=w_up, w_down=w_down)


def reference(tokens, cotangent, expert_ids, route_weights, w_gate, w_up, w_down):
    device_count = N_CTX * N_EXP
    slot_count = TOK_DEV * ROUTES
    per_expert = device_count * CAP
    col_count = D // N_CTX
    route_ids = expert_ids.reshape(device_count, slot_count)
    labels = jnp.arange(EXPERTS, dtype=jnp.int32)
    onehot = (route_ids[:, :, None] == labels[None, None, :]).astype(jnp.int32)
    position = jnp.sum((jnp.cumsum(onehot, axis=1) - 1) * onehot, axis=2)
    source = jnp.arange(device_count, dtype=jnp.int32)[:, None]
    target = (route_ids * per_expert + source * CAP + position).reshape(-1).astype(jnp.int32)
    token_slots = jnp.repeat(tokens, ROUTES, axis=0)
    scaled = (route_weights.reshape(-1, 1) * jnp.repeat(cotangent, ROUTES, axis=0).astype(jnp.float32)).astype(jnp.bfloat16)
    x_buffer = jnp.zeros((EXPERTS * per_expert, D), jnp.bfloat16).at[target].set(token_slots).reshape(EXPERTS, per_expert, D)
    y_buffer = jnp.zeros((EXPERTS * per_expert, D), jnp.bfloat16).at[target].set(scaled).reshape(EXPERTS, per_expert, D)

    def one_expert(bundle):
        slot_x, slot_y, gate_weight, up_weight, down_weight = bundle
        x_blocks = slot_x.reshape(per_expert, N_CTX, col_count).astype(jnp.float32)
        y_blocks = slot_y.reshape(per_expert, N_CTX, col_count).astype(jnp.float32)
        both = jnp.concatenate([gate_weight, up_weight], axis=1).reshape(N_CTX, col_count, 2 * FF).astype(jnp.float32)
        parts = jnp.einsum("rcd,cdf->crf", x_blocks, both).astype(jnp.bfloat16)
        totals = jnp.sum(parts.astype(jnp.float32), axis=0)
        gate_pre = totals[:, :FF]
        up_pre = totals[:, FF:]
        gate_sig = jax.nn.sigmoid(gate_pre)
        hidden = (gate_pre * gate_sig * up_pre).astype(jnp.bfloat16)
        outputs = jnp.dot(hidden, down_weight, preferred_element_type=jnp.float32)
        inner_part = jnp.sum(slot_y.astype(jnp.float32) * outputs, axis=1)
        down_blocks = down_weight.reshape(FF, N_CTX, col_count).astype(jnp.float32)
        back_parts = jnp.einsum("rcd,fcd->crf", y_blocks, down_blocks).astype(jnp.bfloat16)
        back_sum = jnp.sum(back_parts.astype(jnp.float32), axis=0)
        d_up = (back_sum * gate_pre * gate_sig).astype(jnp.bfloat16)
        d_gate = (back_sum * up_pre * gate_sig * (1.0 + gate_pre * (1.0 - gate_sig))).astype(jnp.bfloat16)
        down_grad = jnp.dot(hidden.T, slot_y, preferred_element_type=jnp.float32).astype(jnp.bfloat16)
        gate_grad = jnp.dot(slot_x.T, d_gate, preferred_element_type=jnp.float32).astype(jnp.bfloat16)
        up_grad = jnp.dot(slot_x.T, d_up, preferred_element_type=jnp.float32).astype(jnp.bfloat16)
        slot_grad = (jnp.dot(d_gate, gate_weight.T, preferred_element_type=jnp.float32)
                     + jnp.dot(d_up, up_weight.T, preferred_element_type=jnp.float32)).astype(jnp.bfloat16)
        return gate_grad, up_grad, down_grad, slot_grad, inner_part

    gate_grads, up_grads, down_grads, slot_grads, inner_all = lax.map(
        one_expert, (x_buffer, y_buffer, w_gate, w_up, w_down))
    picked = slot_grads.reshape(EXPERTS * per_expert, D)[target]
    token_grads = jnp.sum(picked.reshape(TOKENS, ROUTES, D).astype(jnp.float32), axis=1).astype(jnp.bfloat16)
    route_grads = inner_all.reshape(-1)[target].reshape(TOKENS, ROUTES) / route_weights
    return token_grads, route_grads, gate_grads, up_grads, down_grads
```

```python
import functools

import jax
import jax.numpy as jnp
from jax import lax
from jax.experimental import pallas as pl
from jax.experimental.pallas import tpu as pltpu
from jax.sharding import PartitionSpec as P

MESH = pl.DeviceIdType.MESH


def slot_table(route_ids, expert_count, capacity):
    labels = jnp.arange(expert_count, dtype=jnp.int32)
    onehot = (route_ids[..., :, None] == labels).astype(jnp.int32)
    position = jnp.sum((jnp.cumsum(onehot, axis=-2) - 1) * onehot, axis=-1)
    target = route_ids * capacity + position
    places = jnp.arange(expert_count * capacity, dtype=jnp.int32)
    return (target[..., None, :] == places[:, None]).astype(jnp.bfloat16)


def forward_hidden(totals, units):
    gate_pre = totals[:, :units]
    up_pre = totals[:, units:]
    gate_sig = jax.nn.sigmoid(gate_pre)
    return (gate_pre * gate_sig * up_pre).astype(jnp.bfloat16)


def backward_grads(totals, back_sum, units):
    gate_pre = totals[:, :units]
    up_pre = totals[:, units:]
    gate_sig = jax.nn.sigmoid(gate_pre)
    d_up = (back_sum * gate_pre * gate_sig).astype(jnp.bfloat16)
    d_gate = (back_sum * up_pre * gate_sig * (1.0 + gate_pre * (1.0 - gate_sig))).astype(
        jnp.bfloat16
    )
    return jnp.concatenate([d_gate, d_up], axis=1)


def body(tokens, cotangent, expert_ids, route_weights, w_gate, w_up, w_down):
    ctx_size = lax.axis_size("ctx")
    exp_size = lax.axis_size("exp")
    tok_count, model_width = tokens.shape
    route_count = expert_ids.shape[1]
    slot_count = tok_count * route_count
    expert_count = w_gate.shape[0] * exp_size
    capacity = max(2, (3 * slot_count + 2 * expert_count - 1) // (2 * expert_count))
    col_count = model_width // ctx_size
    units = w_gate.shape[2]
    row_count = ctx_size * exp_size * capacity
    own_rows = row_count // ctx_size
    all_ids = lax.all_gather(expert_ids, "ctx", axis=0, tiled=True)
    tables = slot_table(all_ids.reshape(ctx_size, slot_count), expert_count, capacity)
    token_slots = jnp.repeat(tokens, route_count, axis=0)
    scaled = (
        route_weights * jnp.repeat(cotangent, route_count, axis=0).astype(jnp.float32)
    ).astype(jnp.bfloat16)
    own_table = lax.dynamic_index_in_dim(tables, lax.axis_index("ctx"), 0, keepdims=False)
    send_x = jnp.dot(own_table, token_slots, preferred_element_type=jnp.float32).astype(
        jnp.bfloat16
    )
    send_y = jnp.dot(own_table, scaled, preferred_element_type=jnp.float32).astype(jnp.bfloat16)
    send_x = send_x.reshape(expert_count, capacity, model_width)
    send_y = send_y.reshape(expert_count, capacity, model_width)
    group_x, group_y = (
        lax.all_to_all(send_x, "exp", split_axis=0, concat_axis=0, tiled=True),
        lax.all_to_all(send_y, "exp", split_axis=0, concat_axis=0, tiled=True),
    )
    slot_x, slot_y = (
        lax.all_to_all(group_x, "ctx", split_axis=2, concat_axis=0, tiled=True),
        lax.all_to_all(group_y, "ctx", split_axis=2, concat_axis=0, tiled=True),
    )
    slot_x = slot_x.reshape(row_count, col_count)
    slot_y = slot_y.reshape(row_count, col_count)
    gate_weight = w_gate[0]
    up_weight = w_up[0]
    down_weight = w_down[0]
    both_weights = jnp.concatenate([gate_weight, up_weight], axis=1)

    def fold_grad(segment):
        gate_acc = lax.dot_general(
            slot_x, segment[:, :units], (((0,), (0,)), ((), ())), preferred_element_type=jnp.float32
        )
        up_acc = lax.dot_general(
            slot_x, segment[:, units:], (((0,), (0,)), ((), ())), preferred_element_type=jnp.float32
        )
        grad_rows = lax.dot_general(
            segment, both_weights, (((1,), (1,)), ((), ())), preferred_element_type=jnp.float32
        )
        return (gate_acc, up_acc, grad_rows)

    row_x, row_y = (
        lax.all_to_all(slot_x, "ctx", split_axis=0, concat_axis=1, tiled=True),
        lax.all_to_all(slot_y, "ctx", split_axis=0, concat_axis=1, tiled=True),
    )
    full_gate, full_up, full_down = (
        lax.all_gather(gate_weight, "ctx", axis=0, tiled=True),
        lax.all_gather(up_weight, "ctx", axis=0, tiled=True),
        lax.all_gather(down_weight, "ctx", axis=1, tiled=True),
    )
    full_both = jnp.concatenate([full_gate, full_up], axis=1).reshape(
        ctx_size, col_count, 2 * units
    )
    gate_blocks = jnp.einsum(
        "rcd,cdf->crf",
        row_x.reshape(own_rows, ctx_size, col_count),
        full_both,
        preferred_element_type=jnp.float32,
    ).astype(jnp.bfloat16)
    totals_own = jnp.sum(gate_blocks.astype(jnp.float32), axis=0)
    hidden_own = forward_hidden(totals_own, units)
    back_blocks = jnp.einsum(
        "rcd,fcd->crf",
        row_y.reshape(own_rows, ctx_size, col_count),
        full_down.reshape(units, ctx_size, col_count),
        preferred_element_type=jnp.float32,
    ).astype(jnp.bfloat16)
    back_own = jnp.sum(back_blocks.astype(jnp.float32), axis=0)
    grads_own = backward_grads(totals_own, back_own, units)
    segment = (
        lax.all_gather(hidden_own, "ctx", axis=0, tiled=True),
        lax.all_gather(grads_own, "ctx", axis=0, tiled=True),
    )
    fold_segment = segment[0]
    outputs = jnp.dot(fold_segment, down_weight, preferred_element_type=jnp.float32)
    inner_rows = jnp.sum(slot_y.astype(jnp.float32) * outputs, axis=1)
    inner_all = inner_rows
    down_acc = lax.dot_general(
        fold_segment, slot_y, (((0,), (0,)), ((), ())), preferred_element_type=jnp.float32
    )
    down_state = (down_acc, inner_all)
    grad_state = fold_grad(segment[1])
    down_acc = down_state[0]
    inner_all = down_state[1]
    gate_acc = grad_state[0]
    up_acc = grad_state[1]
    back_rows = grad_state[2]
    back_slots = back_rows.astype(jnp.bfloat16).reshape(ctx_size, exp_size, capacity, col_count)
    inner_slots = inner_all.reshape(ctx_size, exp_size, capacity)
    home_back = lax.all_to_all(back_slots, "exp", split_axis=1, concat_axis=1, tiled=True)
    home_inner = lax.all_to_all(inner_slots, "exp", split_axis=1, concat_axis=1, tiled=True)
    merged = jnp.einsum(
        "cks,ckd->csd",
        tables,
        home_back.reshape(ctx_size, expert_count * capacity, col_count),
        preferred_element_type=jnp.float32,
    )
    merged = jnp.sum(merged.reshape(ctx_size, tok_count, route_count, col_count), axis=2).astype(
        jnp.bfloat16
    )
    grads_home = lax.all_to_all(merged, "ctx", split_axis=0, concat_axis=2, tiled=True)
    token_grads = grads_home.reshape(tok_count, model_width)
    inner_home = jnp.einsum(
        "cks,ck->cs",
        tables.astype(jnp.float32),
        home_inner.reshape(ctx_size, expert_count * capacity),
        precision=lax.Precision.HIGHEST,
    )
    route_sums = lax.psum_scatter(inner_home, "ctx", scatter_dimension=0, tiled=True).reshape(
        tok_count, route_count
    )
    route_grads = route_sums / route_weights
    gate_grads = gate_acc.astype(jnp.bfloat16)[None]
    up_grads = up_acc.astype(jnp.bfloat16)[None]
    down_grads = down_acc.astype(jnp.bfloat16)[None]
    return (token_grads, route_grads, gate_grads, up_grads, down_grads)


def ctx_neighbours(me):
    sib = me + 1 - 2 * (me % 2)
    across = me + 2 - 4 * ((me // 2) % 2)
    along = me + 4 - 8 * ((me // 4) % 2)
    return sib, across, along


def enter(ctx_peers, exp_peers):
    barrier = pltpu.get_barrier_semaphore()
    for peer in ctx_peers:
        pl.semaphore_signal(barrier, inc=1, device_id={"ctx": peer}, device_id_type=MESH)
    for peer in exp_peers:
        pl.semaphore_signal(barrier, inc=1, device_id={"exp": peer}, device_id_type=MESH)
    pl.semaphore_wait(barrier, len(ctx_peers) + len(exp_peers))


class Gather:
    def __init__(self, own, out, send_sem, recv_sem):
        me = lax.axis_index("ctx")
        sib, across, along = ctx_neighbours(me)
        half = own.shape[0] // 2
        first, second = pl.ds(0, half), pl.ds(half, half)
        far = ctx_neighbours(across)[2]

        def copy(k, source, target, peer):
            return pltpu.make_async_remote_copy(
                src_ref=source,
                dst_ref=target,
                send_sem=send_sem.at[k],
                recv_sem=recv_sem.at[k],
                device_id={"ctx": peer},
                device_id_type=MESH,
            )

        self.c = [
            copy(0, own.at[first], out.at[me, first], across),
            copy(1, own.at[second], out.at[me, second], along),
            copy(2, own.at[second], out.at[me, second], across),
            copy(3, own.at[first], out.at[me, first], along),
            copy(4, own, out.at[me], sib),
            copy(5, out.at[across, first], out.at[across, first], along),
            copy(6, out.at[along, second], out.at[along, second], across),
            copy(7, out.at[across], out.at[across], sib),
            copy(8, out.at[along], out.at[along], sib),
            copy(9, out.at[far, first], out.at[far, first], sib),
            copy(10, out.at[far, second], out.at[far, second], sib),
        ]

    def start(self, *which):
        for k in which:
            self.c[k].start()

    def arrived(self, *which):
        for k in which:
            self.c[k].wait_recv()

    def relay(self):
        self.arrived(0)
        self.start(5)
        self.arrived(1)
        self.start(6)

    def share_near(self):
        self.arrived(2)
        self.start(7)
        self.arrived(3)
        self.start(8)

    def share_far(self):
        self.arrived(5)
        self.start(9)
        self.arrived(6)
        self.start(10)

    def sent(self):
        for one in self.c:
            one.wait_send()


class Scatter:
    def __init__(self, one, two, got_one, got_two, send_sem, recv_sem):
        sib, across, along = ctx_neighbours(lax.axis_index("ctx"))
        self.one, self.two, self.got_one, self.got_two = one, two, got_one, got_two

        def copy(k, source, target, peer):
            return pltpu.make_async_remote_copy(
                src_ref=source,
                dst_ref=target,
                send_sem=send_sem.at[k],
                recv_sem=recv_sem.at[k],
                device_id={"ctx": peer},
                device_id_type=MESH,
            )

        self.c = [
            copy(0, one.at[0], got_one.at[0], across),
            copy(1, one.at[1], got_one.at[1], along),
            copy(2, two.at[0], got_two.at[0], along),
            copy(3, two.at[1], got_two.at[1], across),
        ]

    def first(self, term, chips, keep):
        own, across, along, far = chips
        bf = self.one.dtype
        half = self.one.shape[2]
        part = term(far)
        self.one[0, 1] = part[:half].astype(bf)
        self.one[1, 1] = part[half:].astype(bf)
        part = term(across)
        self.one[0, 0] = part[:half].astype(bf)
        keep[3 * half:4 * half] = part[half:]
        self.c[0].start()
        part = term(along)
        self.one[1, 0] = part[half:].astype(bf)
        keep[2 * half:3 * half] = part[:half]
        self.c[1].start()
        keep[:2 * half] = term(own)

    def second(self, keep):
        bf, f32 = self.one.dtype, jnp.float32
        half = self.one.shape[2]
        self.c[0].wait_recv()
        self.two[0] = (keep[2 * half:3 * half] + self.got_one[0, 1].astype(f32)).astype(bf)
        self.c[2].start()
        self.c[1].wait_recv()
        self.two[1] = (keep[3 * half:4 * half] + self.got_one[1, 1].astype(f32)).astype(bf)
        self.c[3].start()

    def total(self, keep):
        f32 = jnp.float32
        half = self.one.shape[2]
        self.c[2].wait_recv()
        upper = keep[:half] + self.got_one[0, 0].astype(f32) + self.got_two[0].astype(f32)
        self.c[3].wait_recv()
        lower = keep[half:2 * half] + self.got_one[1, 0].astype(f32) + self.got_two[1].astype(f32)
        return upper, lower

    def sent(self):
        for one in self.c:
            one.wait_send()


NT = (((1,), (1,)), ((), ()))
TN = (((0,), (0,)), ((), ()))
NN = (((1,), (0,)), ((), ()))


def dot(a, b, dims):
    return lax.dot_general(a, b, dims, preferred_element_type=jnp.float32)


def kernel(
    n_exp, n_ctx, cap,
    tok_in, cot_in, ids_row, weight_row, w_gate, w_up, w_down,
    token_out, route_out, gate_grad, up_grad, down_grad,
    send_x, send_y, x_rows, y_rows, gate_w, up_w, down_w, table,
    gate_acc, up_acc, back_acc, hid_two, dg_two, du_two, x_two, y_two,
    back, inner, home, home_inner, keep, s_one, s_two, s_got_one, s_got_two,
    w_send, w_recv, w_local, d_send, d_recv, d_local,
    c_send, c_recv, c_local, t_send, t_recv, s_send, s_recv,
    r_send, r_recv, r_local,
    tok, cot, in_sem,
):
    me_exp = lax.axis_index("exp")
    me = lax.axis_index("ctx")
    bf, f32 = jnp.bfloat16, jnp.float32
    sib, across, along = ctx_neighbours(me)
    far = ctx_neighbours(across)[2]
    core = lax.rem(me, 2)
    n_chip = n_ctx // 2
    exp_peers = [lax.rem(me_exp + d, n_exp) for d in range(1, n_exp)]
    loads = [
        pltpu.make_async_copy(tok_in, tok, in_sem.at[0]),
        pltpu.make_async_copy(cot_in, cot, in_sem.at[1]),
    ]
    for one in loads:
        one.start()
    enter([sib, across, along], exp_peers)

    weights = [
        Gather(own.at[0], out, w_send.at[i], w_recv.at[i])
        for i, (own, out) in enumerate(((w_gate, gate_w), (w_up, up_w), (w_down, down_w)))
    ]
    own_weights = [
        pltpu.make_async_copy(own.at[0], out.at[me], w_local.at[i])
        for i, (own, out) in enumerate(((w_gate, gate_w), (w_up, up_w), (w_down, down_w)))
    ]
    for g in weights:
        g.start(0, 1)
    for g in weights:
        g.start(2, 3)

    count, width = tok.shape
    cols = width // n_ctx
    rows = n_exp * cap
    units = gate_acc.shape[1]

    def rows_of(at):
        return pl.ds(pl.multiple_of(at * cap, cap), cap)

    def columns(at):
        return pl.ds(pl.multiple_of(at * cols, cols), cols)

    mine = pl.ds(pl.multiple_of(core * rows, rows), rows)

    down_i = lax.broadcasted_iota(jnp.int32, (count, count), 0)
    over_i = lax.broadcasted_iota(jnp.int32, (count, count), 1)
    row = ids_row[...]
    diagonal = down_i == over_i
    row_f = row.astype(f32)
    col_f = jnp.sum(jnp.where(diagonal, row_f, 0.0), axis=1, keepdims=True)
    weight_col = jnp.sum(jnp.where(diagonal, weight_row[...], 0.0), axis=1, keepdims=True)
    position = jnp.sum(
        jnp.where((col_f == row_f) & (down_i < over_i), 1.0, 0.0), axis=0, keepdims=True
    )
    target = row * cap + position.astype(jnp.int32)
    places = lax.broadcasted_iota(jnp.int32, (n_exp * cap, count), 0)
    table[...] = jnp.where(places == target, 1.0, 0.0).astype(bf)

    def exchange(source, out, sends, recvs, local, which):
        moves = [
            pltpu.make_async_remote_copy(
                src_ref=source.at[rows_of(peer)],
                dst_ref=out.at[rows_of(me_exp)],
                send_sem=sends.at[d, which],
                recv_sem=recvs.at[d, which],
                device_id={"exp": peer},
                device_id_type=MESH,
            )
            for d, peer in enumerate(exp_peers)
        ]
        moves.append(
            pltpu.make_async_copy(
                source.at[rows_of(me_exp)], out.at[rows_of(me_exp)], local.at[which]
            )
        )
        for one in moves:
            one.start()
        return moves

    loads[0].wait()
    send_x[...] = dot(table[...], tok[...], NN).astype(bf)
    sent_x = exchange(send_x, x_rows, d_send, d_recv, d_local, 0)
    loads[1].wait()
    scaled = (weight_col * cot[...].astype(f32)).astype(bf)
    send_y[...] = dot(table[...], scaled, NN).astype(bf)
    sent_y = exchange(send_y, y_rows, d_send, d_recv, d_local, 1)
    for g, one in zip(weights, own_weights):
        g.start(4)
        one.start()
    for g in weights:
        g.relay()
    for g in weights:
        g.share_near()

    def pair(source, out, which):
        moves = []
        for q in range(n_chip):
            moves.append(
                pltpu.make_async_remote_copy(
                    src_ref=source.at[:, columns(2 * q + 1 - core)],
                    dst_ref=out.at[q, mine],
                    send_sem=c_send.at[which, q],
                    recv_sem=c_recv.at[which, q],
                    device_id={"ctx": sib},
                    device_id_type=MESH,
                )
            )
            moves.append(
                pltpu.make_async_copy(
                    source.at[:, columns(2 * q + core)], out.at[q, mine], c_local.at[which, q]
                )
            )
        for one in moves:
            one.start()
        return moves

    def tell(out, which):
        one = pltpu.make_async_remote_copy(
            src_ref=out.at[mine],
            dst_ref=out.at[mine],
            send_sem=t_send.at[which],
            recv_sem=t_recv.at[which],
            device_id={"ctx": sib},
            device_id_type=MESH,
        )
        one.start()
        return one

    def forward_x(c, start=False):
        xc = x_rows[:, columns(c)]
        for acc, weight in ((gate_acc, gate_w), (up_acc, up_w)):
            part = dot(xc, weight[c], NN)
            acc[...] = part if start else acc[...] + part

    def forward_y(c, start=False):
        part = dot(y_rows[:, columns(c)], down_w[c], NT)
        back_acc[...] = part if start else back_acc[...] + part

    near = (sib, across, along, ctx_neighbours(across)[0], ctx_neighbours(along)[0])
    last = ctx_neighbours(far)[0]
    for one in sent_x:
        one.wait()
    paired_x = pair(x_rows, x_two, 0)
    for one in own_weights:
        one.wait()
    forward_x(me, True)
    for g in weights[:2]:
        g.arrived(4)
        g.arrived(7, 8)
    for c in near:
        forward_x(c)
    for g in weights[:2]:
        g.share_far()
    forward_x(far)
    for g in weights[:2]:
        g.arrived(9, 10)
    forward_x(last)

    gate, up = gate_acc[...], up_acc[...]
    sig = 1.0 / (1.0 + jnp.exp(-gate))
    hid_two[mine] = (gate * sig * up).astype(bf)
    told = [tell(hid_two, 0)]

    for one in sent_y:
        one.wait()
    paired_y = pair(y_rows, y_two, 1)
    weights[2].share_far()
    weights[2].arrived(4)
    weights[2].arrived(7, 8)
    forward_y(me, True)
    for c in near:
        forward_y(c)

    chips = [lax.div(at, 2) for at in (me, across, along, far)]
    sums = [
        Scatter(
            s_one.at[i], s_two.at[i], s_got_one.at[i], s_got_two.at[i], s_send.at[i], s_recv.at[i]
        )
        for i in range(3)
    ]
    told[0].wait()
    for one in paired_y:
        one.wait()
    sums[0].first(lambda q: dot(y_two[q], hid_two[...], TN), chips, keep.at[0])

    forward_y(far)
    weights[2].arrived(9, 10)
    forward_y(last)
    gate, up, back_sum = gate_acc[...], up_acc[...], back_acc[...]
    sig = 1.0 / (1.0 + jnp.exp(-gate))
    dg_two[mine] = (back_sum * up * sig * (1.0 + gate * (1.0 - sig))).astype(bf)
    told.append(tell(dg_two, 1))
    du_two[mine] = (back_sum * gate * sig).astype(bf)
    told.append(tell(du_two, 2))
    inner[...] = jnp.broadcast_to(
        jnp.sum(hid_two[mine].astype(f32) * back_sum, axis=1, keepdims=True), inner.shape
    )
    sent_inner = exchange(inner, home_inner, r_send, r_recv, r_local, 0)
    for one in paired_x:
        one.wait()
    told[1].wait()
    sums[1].first(lambda q: dot(x_two[q], dg_two[...], TN), chips, keep.at[1])
    told[2].wait()
    sums[2].first(lambda q: dot(x_two[q], du_two[...], TN), chips, keep.at[2])
    sums[0].second(keep.at[0])
    for c in range(n_ctx):
        back[:, c * cols:(c + 1) * cols] = (
            dot(dg_two[mine], gate_w[c], NT) + dot(du_two[mine], up_w[c], NT)
        ).astype(bf)
    sent_back = exchange(back, home, r_send, r_recv, r_local, 1)
    sums[1].second(keep.at[1])
    upper, lower = sums[0].total(keep.at[0])
    half = cols // 2
    down_grad[:, :half] = upper.T.astype(bf)
    down_grad[:, half:] = lower.T.astype(bf)
    for one in sent_inner + sent_back:
        one.wait()
    token_out[...] = dot(table[...], home[...], TN).astype(bf)
    route_out[...] = (
        jnp.sum(table[...].astype(f32) * home_inner[...], axis=0, keepdims=True) / weight_row[...]
    )
    sums[2].second(keep.at[2])
    for i, out in ((1, gate_grad), (2, up_grad)):
        upper, lower = sums[i].total(keep.at[i])
        out[:half] = upper.astype(bf)
        out[half:] = lower.astype(bf)
    for g in weights + sums:
        g.sent()


def hand_over(*refs):
    for source, out in zip(refs[:5], refs[5:]):
        out[...] = source[...]


def fast_body(tokens, cotangent, expert_ids, route_weights, w_gate, w_up, w_down):
    n_ctx = lax.axis_size("ctx")
    n_exp = lax.axis_size("exp")
    count, width = tokens.shape
    cap = max(2, (3 * count + 2 * n_exp - 1) // (2 * n_exp))
    cols = width // n_ctx
    units = w_gate.shape[2]
    rows = n_exp * cap
    half = cols // 2
    bf, f32 = jnp.bfloat16, jnp.float32
    vm = pl.BlockSpec(memory_space=pltpu.VMEM)
    hbm = pl.BlockSpec(memory_space=pl.ANY)
    dma = pltpu.SemaphoreType.DMA
    token_grads, route, gate_grads, up_grads, down_grads = pl.pallas_call(
        functools.partial(kernel, n_exp, n_ctx, cap),
        out_shape=(
            jax.ShapeDtypeStruct((count, width), bf),
            jax.ShapeDtypeStruct((1, count), f32),
            jax.ShapeDtypeStruct((cols, units), bf),
            jax.ShapeDtypeStruct((cols, units), bf),
            jax.ShapeDtypeStruct((units, cols), bf),
        ),
        in_specs=[hbm] * 2 + [vm] * 2 + [hbm] * 3,
        out_specs=(vm,) * 5,
        scratch_shapes=[pltpu.VMEM((rows, width), bf)] * 4
        + [
            pltpu.VMEM((n_ctx, cols, units), bf),
            pltpu.VMEM((n_ctx, cols, units), bf),
            pltpu.VMEM((n_ctx, units, cols), bf),
            pltpu.VMEM((rows, count), bf),
        ]
        + [pltpu.VMEM((rows, units), f32)] * 3
        + [pltpu.VMEM((2 * rows, units), bf)] * 3
        + [pltpu.VMEM((n_ctx // 2, 2 * rows, cols), bf)] * 2
        + [
            pltpu.VMEM((rows, width), bf),
            pltpu.VMEM((rows, count), f32),
            pltpu.VMEM((rows, width), bf),
            pltpu.VMEM((rows, count), f32),
            pltpu.VMEM((3, 4 * half, units), f32),
            pltpu.VMEM((3, 2, 2, half, units), bf),
            pltpu.VMEM((3, 2, half, units), bf),
            pltpu.VMEM((3, 2, 2, half, units), bf),
            pltpu.VMEM((3, 2, half, units), bf),
        ]
        + [
            dma((3, 11)), dma((3, 11)), dma((3,)),
            dma((n_exp - 1, 2)), dma((n_exp - 1, 2)), dma((2,)),
            dma((2, n_ctx // 2)), dma((2, n_ctx // 2)), dma((2, n_ctx // 2)),
            dma((3,)), dma((3,)), dma((3, 4)), dma((3, 4)),
            dma((n_exp - 1, 2)), dma((n_exp - 1, 2)), dma((2,)),
            pltpu.VMEM((count, width), bf), pltpu.VMEM((count, width), bf), dma((2,)),
        ],
        compiler_params=pltpu.CompilerParams(
            collective_id=0, has_side_effects=True, vmem_limit_bytes=56 * 1024 * 1024
        ),
    )(
        tokens, cotangent, expert_ids.reshape(1, count), route_weights.reshape(1, count),
        w_gate, w_up, w_down,
    )
    results = (token_grads, route, gate_grads, up_grads, down_grads)
    token_grads, route, gate_grads, up_grads, down_grads = pl.pallas_call(
        hand_over,
        out_shape=tuple(jax.ShapeDtypeStruct(r.shape, r.dtype) for r in results),
        in_specs=[vm] * 5,
        out_specs=(vm,) * 5,
    )(*results)
    return (
        token_grads, route.reshape(count, 1), gate_grads[None], up_grads[None], down_grads[None]
    )


def solution(mesh):
    return jax.shard_map(
        fast_body if mesh.shape["ctx"] == 8 else body,
        mesh=mesh,
        in_specs=(
            P(("ctx", "exp"), None),
            P(("ctx", "exp"), None),
            P(("ctx", "exp"), None),
            P(("ctx", "exp"), None),
            P("exp", "ctx", None),
            P("exp", "ctx", None),
            P("exp", None, "ctx"),
        ),
        out_specs=(
            P(("ctx", "exp"), None),
            P(("ctx", "exp"), None),
            P("exp", "ctx", None),
            P("exp", "ctx", None),
            P("exp", None, "ctx"),
        ),
        check_vma=False,
    )
```

```python
import functools

import jax
import jax.numpy as jnp
from jax import lax
from jax.experimental import pallas as pl
from jax.experimental.pallas import tpu as pltpu
from jax.sharding import PartitionSpec as P

MESH = pl.DeviceIdType.MESH


def slot_table(route_ids, expert_count, capacity):
    labels = jnp.arange(expert_count, dtype=jnp.int32)
    onehot = (route_ids[..., :, None] == labels).astype(jnp.int32)
    position = jnp.sum((jnp.cumsum(onehot, axis=-2) - 1) * onehot, axis=-1)
    target = route_ids * capacity + position
    places = jnp.arange(expert_count * capacity, dtype=jnp.int32)
    return (target[..., None, :] == places[:, None]).astype(jnp.bfloat16)


def forward_hidden(totals, units):
    gate_pre = totals[:, :units]
    up_pre = totals[:, units:]
    gate_sig = jax.nn.sigmoid(gate_pre)
    return (gate_pre * gate_sig * up_pre).astype(jnp.bfloat16)


def backward_grads(totals, back_sum, units):
    gate_pre = totals[:, :units]
    up_pre = totals[:, units:]
    gate_sig = jax.nn.sigmoid(gate_pre)
    d_up = (back_sum * gate_pre * gate_sig).astype(jnp.bfloat16)
    d_gate = (back_sum * up_pre * gate_sig * (1.0 + gate_pre * (1.0 - gate_sig))).astype(
        jnp.bfloat16
    )
    return jnp.concatenate([d_gate, d_up], axis=1)


def body(tokens, cotangent, expert_ids, route_weights, w_gate, w_up, w_down):
    ctx_size = lax.axis_size("ctx")
    exp_size = lax.axis_size("exp")
    tok_count, model_width = tokens.shape
    route_count = expert_ids.shape[1]
    slot_count = tok_count * route_count
    expert_count = w_gate.shape[0] * exp_size
    capacity = max(2, (3 * slot_count + 2 * expert_count - 1) // (2 * expert_count))
    col_count = model_width // ctx_size
    units = w_gate.shape[2]
    row_count = ctx_size * exp_size * capacity
    own_rows = row_count // ctx_size
    all_ids = lax.all_gather(expert_ids, "ctx", axis=0, tiled=True)
    tables = slot_table(all_ids.reshape(ctx_size, slot_count), expert_count, capacity)
    token_slots = jnp.repeat(tokens, route_count, axis=0)
    scaled = (
        route_weights * jnp.repeat(cotangent, route_count, axis=0).astype(jnp.float32)
    ).astype(jnp.bfloat16)
    own_table = lax.dynamic_index_in_dim(tables, lax.axis_index("ctx"), 0, keepdims=False)
    send_x = jnp.dot(own_table, token_slots, preferred_element_type=jnp.float32).astype(
        jnp.bfloat16
    )
    send_y = jnp.dot(own_table, scaled, preferred_element_type=jnp.float32).astype(jnp.bfloat16)
    send_x = send_x.reshape(expert_count, capacity, model_width)
    send_y = send_y.reshape(expert_count, capacity, model_width)
    group_x, group_y = (
        lax.all_to_all(send_x, "exp", split_axis=0, concat_axis=0, tiled=True),
        lax.all_to_all(send_y, "exp", split_axis=0, concat_axis=0, tiled=True),
    )
    slot_x, slot_y = (
        lax.all_to_all(group_x, "ctx", split_axis=2, concat_axis=0, tiled=True),
        lax.all_to_all(group_y, "ctx", split_axis=2, concat_axis=0, tiled=True),
    )
    slot_x = slot_x.reshape(row_count, col_count)
    slot_y = slot_y.reshape(row_count, col_count)
    gate_weight = w_gate[0]
    up_weight = w_up[0]
    down_weight = w_down[0]
    both_weights = jnp.concatenate([gate_weight, up_weight], axis=1)

    def fold_grad(segment):
        gate_acc = lax.dot_general(
            slot_x, segment[:, :units], (((0,), (0,)), ((), ())), preferred_element_type=jnp.float32
        )
        up_acc = lax.dot_general(
            slot_x, segment[:, units:], (((0,), (0,)), ((), ())), preferred_element_type=jnp.float32
        )
        grad_rows = lax.dot_general(
            segment, both_weights, (((1,), (1,)), ((), ())), preferred_element_type=jnp.float32
        )
        return (gate_acc, up_acc, grad_rows)

    row_x, row_y = (
        lax.all_to_all(slot_x, "ctx", split_axis=0, concat_axis=1, tiled=True),
        lax.all_to_all(slot_y, "ctx", split_axis=0, concat_axis=1, tiled=True),
    )
    full_gate, full_up, full_down = (
        lax.all_gather(gate_weight, "ctx", axis=0, tiled=True),
        lax.all_gather(up_weight, "ctx", axis=0, tiled=True),
        lax.all_gather(down_weight, "ctx", axis=1, tiled=True),
    )
    full_both = jnp.concatenate([full_gate, full_up], axis=1).reshape(
        ctx_size, col_count, 2 * units
    )
    gate_blocks = jnp.einsum(
        "rcd,cdf->crf",
        row_x.reshape(own_rows, ctx_size, col_count),
        full_both,
        preferred_element_type=jnp.float32,
    ).astype(jnp.bfloat16)
    totals_own = jnp.sum(gate_blocks.astype(jnp.float32), axis=0)
    hidden_own = forward_hidden(totals_own, units)
    back_blocks = jnp.einsum(
        "rcd,fcd->crf",
        row_y.reshape(own_rows, ctx_size, col_count),
        full_down.reshape(units, ctx_size, col_count),
        preferred_element_type=jnp.float32,
    ).astype(jnp.bfloat16)
    back_own = jnp.sum(back_blocks.astype(jnp.float32), axis=0)
    grads_own = backward_grads(totals_own, back_own, units)
    segment = (
        lax.all_gather(hidden_own, "ctx", axis=0, tiled=True),
        lax.all_gather(grads_own, "ctx", axis=0, tiled=True),
    )
    fold_segment = segment[0]
    outputs = jnp.dot(fold_segment, down_weight, preferred_element_type=jnp.float32)
    inner_rows = jnp.sum(slot_y.astype(jnp.float32) * outputs, axis=1)
    inner_all = inner_rows
    down_acc = lax.dot_general(
        fold_segment, slot_y, (((0,), (0,)), ((), ())), preferred_element_type=jnp.float32
    )
    down_state = (down_acc, inner_all)
    grad_state = fold_grad(segment[1])
    down_acc = down_state[0]
    inner_all = down_state[1]
    gate_acc = grad_state[0]
    up_acc = grad_state[1]
    back_rows = grad_state[2]
    back_slots = back_rows.astype(jnp.bfloat16).reshape(ctx_size, exp_size, capacity, col_count)
    inner_slots = inner_all.reshape(ctx_size, exp_size, capacity)
    home_back = lax.all_to_all(back_slots, "exp", split_axis=1, concat_axis=1, tiled=True)
    home_inner = lax.all_to_all(inner_slots, "exp", split_axis=1, concat_axis=1, tiled=True)
    merged = jnp.einsum(
        "cks,ckd->csd",
        tables,
        home_back.reshape(ctx_size, expert_count * capacity, col_count),
        preferred_element_type=jnp.float32,
    )
    merged = jnp.sum(merged.reshape(ctx_size, tok_count, route_count, col_count), axis=2).astype(
        jnp.bfloat16
    )
    grads_home = lax.all_to_all(merged, "ctx", split_axis=0, concat_axis=2, tiled=True)
    token_grads = grads_home.reshape(tok_count, model_width)
    inner_home = jnp.einsum(
        "cks,ck->cs",
        tables.astype(jnp.float32),
        home_inner.reshape(ctx_size, expert_count * capacity),
        precision=lax.Precision.HIGHEST,
    )
    route_sums = lax.psum_scatter(inner_home, "ctx", scatter_dimension=0, tiled=True).reshape(
        tok_count, route_count
    )
    route_grads = route_sums / route_weights
    gate_grads = gate_acc.astype(jnp.bfloat16)[None]
    up_grads = up_acc.astype(jnp.bfloat16)[None]
    down_grads = down_acc.astype(jnp.bfloat16)[None]
    return (token_grads, route_grads, gate_grads, up_grads, down_grads)


def ctx_neighbours(me):
    sib = me + 1 - 2 * (me % 2)
    across = me + 2 - 4 * ((me // 2) % 2)
    along = me + 4 - 8 * ((me // 4) % 2)
    return sib, across, along


def greet(ctx_peers, exp_peers):
    barrier = pltpu.get_barrier_semaphore()
    for peer in ctx_peers:
        pl.semaphore_signal(barrier, inc=1, device_id={"ctx": peer}, device_id_type=MESH)
    for peer in exp_peers:
        pl.semaphore_signal(barrier, inc=1, device_id={"exp": peer}, device_id_type=MESH)
    return len(ctx_peers) + len(exp_peers)


class Copies:
    def __init__(self, send_sem, recv_sem, local_sem):
        self.sems = send_sem, recv_sem, local_sem
        self.far, self.near = [], 0

    def remote(self, source, target, **peer):
        k = len(self.far)
        one = pltpu.make_async_remote_copy(
            src_ref=source,
            dst_ref=target,
            send_sem=self.sems[0].at[k],
            recv_sem=self.sems[1].at[k],
            device_id=peer,
            device_id_type=MESH,
        )
        self.far.append(one)
        return one

    def local(self, source, target):
        one = pltpu.make_async_copy(source, target, self.sems[2].at[self.near])
        self.near += 1
        return one

    def sent(self):
        for one in self.far:
            one.wait_send()


def begin(copies):
    for one in copies:
        one.start()


def arrived(copies):
    for one in copies:
        one.wait_recv()


NT = (((1,), (1,)), ((), ()))
TN = (((0,), (0,)), ((), ()))
NN = (((1,), (0,)), ((), ()))


def dot(a, b, dims):
    return lax.dot_general(a, b, dims, preferred_element_type=jnp.float32)


def kernel(
    n_exp, n_ctx, cap,
    tok_in, cot_in, ids_row, weight_row, w_gate, w_up, w_down,
    token_out, route_out, gate_grad, up_grad, down_grad,
    tok, cot, scaled, scaled_far, ids_far, table, send_x, x_rows, send_y, y_rows,
    gate_w, up_w, down_w, gate_t, up_t, down_t,
    pre_send, pre_got, pre, back_send, back_got, hid_all, d_all, x_two, y_two,
    back, home, inner, home_inner,
    keep, sum_send, sum_got, keep_down, down_send, down_got, tok_send, tok_got,
    send_sem, recv_sem, local_sem,
):
    me_exp = lax.axis_index("exp")
    me = lax.axis_index("ctx")
    bf, f32 = jnp.bfloat16, jnp.float32
    sib, across, along = ctx_neighbours(me)
    core = lax.rem(me, 2)
    side_x = lax.rem(lax.div(me, 2), 2)
    side_y = lax.div(me, 4)
    exp_peers = [lax.rem(me_exp + d, n_exp) for d in range(1, n_exp)]
    count, width = cot.shape
    cols = width // n_ctx
    rows = n_exp * cap
    wide, strip = width // 2, width // 4

    def cut(at, size):
        return pl.ds(pl.multiple_of(at * size, size), size)

    def part(base, size):
        return pl.ds(pl.multiple_of(base, 16), size)

    copies = Copies(send_sem, recv_sem, local_sem)
    remote, local = copies.remote, copies.local
    block, other = cut(side_y, wide), cut(1 - side_y, wide)
    loads = [local(cot_in, cot), local(tok_in.at[:, block], tok.at[0])]
    begin(loads)
    greeted = greet([sib, across, along], exp_peers)

    down_i = lax.broadcasted_iota(jnp.int32, (count, count), 0)
    over_i = lax.broadcasted_iota(jnp.int32, (count, count), 1)
    diagonal = down_i == over_i

    def fill_table(at, row):
        row_f = row.astype(f32)
        col_f = jnp.sum(jnp.where(diagonal, row_f, 0.0), axis=1, keepdims=True)
        position = jnp.sum(
            jnp.where((col_f == row_f) & (down_i < over_i), 1.0, 0.0), axis=0, keepdims=True
        )
        target = row * cap + position.astype(jnp.int32)
        places = lax.broadcasted_iota(jnp.int32, (rows, count), 0)
        table[at] = jnp.where(places == target, 1.0, 0.0).astype(bf)

    def place(at):
        return (lax.rem(at, 2) * 2 + lax.div(at, 2)) * cap

    def scatter(source, out, base):
        moves = [
            remote(
                source.at[part(base + peer * cap, cap)],
                out.at[part(base + place(me_exp), cap)],
                exp=peer,
            )
            for peer in exp_peers
        ]
        moves.append(
            local(
                source.at[part(base + me_exp * cap, cap)],
                out.at[part(base + place(me_exp), cap)],
            )
        )
        return moves

    def give_back(source, out, base, peers, own):
        moves = [
            remote(
                source.at[part(base + place(peer), cap)],
                out.at[part(base + me_exp * cap, cap)],
                exp=peer,
            )
            for peer in peers
        ]
        if own:
            moves.append(
                local(
                    source.at[part(base + place(me_exp), cap)],
                    out.at[part(base + me_exp * cap, cap)],
                )
            )
        begin(moves)
        return moves

    fill_table(0, ids_row[...])
    weight_col = jnp.sum(jnp.where(diagonal, weight_row[...], 0.0), axis=1, keepdims=True)
    loads[0].wait()
    scaled[...] = (weight_col * cot[...].astype(f32)).astype(bf)
    loads[1].wait()
    send_x[:rows] = dot(table[0], tok[0], NN).astype(bf)

    def gathered(own, out, at, at_peer, peer):
        return (
            remote(own.at[0], out.at[at], ctx=peer),
            remote(own.at[0], out.at[at], ctx=sib),
            remote(out.at[at_peer], out.at[at_peer], ctx=sib),
            local(own.at[0], out.at[at]),
        )

    at, at_across = cut(lax.rem(me, 4), cols), cut(lax.rem(across, 4), cols)
    side_w = [gathered(own, out, at, at_across, across) for own, out in ((w_gate, gate_w), (w_up, up_w))]
    side_w.append(gathered(w_down, down_w, side_y * 2 + core, (1 - side_y) * 2 + core, along))
    spread_x = [
        remote(ids_row, ids_far.at[0], ctx=along),
        remote(tok_in.at[:, other], tok.at[1], ctx=along),
    ]
    spread_y = [remote(ids_row, ids_far.at[1], ctx=across)] + [
        remote(
            scaled.at[:, cut(2 * s + 1 - side_x, strip)],
            scaled_far.at[:, s * strip:(s + 1) * strip],
            ctx=across,
        )
        for s in range(2)
    ]
    sent_x = [scatter(send_x, x_rows, base) for base in (0, rows)]
    sent_y = [scatter(send_y, y_rows, base) for base in (0, rows)]
    pl.semaphore_wait(pltpu.get_barrier_semaphore(), greeted)
    begin(spread_x)
    begin(spread_y)
    begin(sent_x[0])
    for g in side_w:
        g[0].start()
    for g in side_w:
        begin(g[1::2])
    for s in range(2):
        send_y[:rows, s * strip:(s + 1) * strip] = dot(
            table[0], scaled[:, cut(2 * s + side_x, strip)], NN
        ).astype(bf)
    spread_x[0].wait_recv()
    fill_table(1, ids_far[0])
    spread_x[1].wait_recv()
    send_x[rows:] = dot(table[1], tok[1], NN).astype(bf)
    begin(sent_x[1])
    spread_y[0].wait_recv()
    fill_table(2, ids_far[1])
    arrived(spread_y[1:])
    send_y[rows:] = dot(table[2], scaled_far[...], NN).astype(bf)
    begin(sent_y[1])
    begin(sent_y[0])

    def all_here(g):
        g[3].wait()
        g[1].wait_recv()
        g[2].wait_recv()

    def pass_on(g):
        g[0].wait_recv()
        g[2].start()

    pre_moves = [remote(pre_send.at[m], pre_got.at[m], ctx=along) for m in (0, 1)]
    pass_on(side_w[0])
    pass_on(side_w[2])
    arrived(sent_x[0])
    all_here(side_w[0])
    pre[0] = dot(x_rows[:rows], gate_w[...], NN)
    arrived(sent_x[1])
    pre_send[0] = dot(x_rows[rows:], gate_w[...], NN).astype(bf)
    pre_moves[0].start()
    pair = cut(core, 2 * rows)

    def pair_up(source, out):
        moves = []
        for q in range(2):
            moves.append(
                remote(source.at[:, cut(2 * q + 1 - core, cols)], out.at[q, pair], ctx=sib)
            )
            moves.append(local(source.at[:, cut(2 * q + core, cols)], out.at[q, pair]))
        begin(moves)
        return moves

    paired_x = pair_up(x_rows, x_two)
    all_here(side_w[2])
    for q in range(4):
        down_t[q * cols:(q + 1) * cols] = down_w[q].T
    pass_on(side_w[1])
    all_here(side_w[1])
    pre_send[1] = dot(x_rows[rows:], up_w[...], NN).astype(bf)
    pre_moves[1].start()
    pre[1] = dot(x_rows[:rows], up_w[...], NN)
    back_move = remote(back_send, back_got, ctx=across)
    arrived(sent_y[1])
    back_send[...] = dot(y_rows[rows:], down_t[...], NN).astype(bf)
    back_move.start()
    gate_t[...] = gate_w[...].T
    up_t[...] = up_w[...].T

    ours = part(core * 2 * rows, rows)
    theirs = part(core * 2 * rows + rows, rows)
    pre_moves[0].wait_recv()
    pre[0] = pre[0] + pre_got[0].astype(f32)
    pre_moves[1].wait_recv()
    pre[1] = pre[1] + pre_got[1].astype(f32)
    gate, up = pre[0], pre[1]
    sig = 1.0 / (1.0 + jnp.exp(-gate))
    hidden = (gate * sig * up).astype(bf)
    hid_all[ours] = hidden
    hid_across = remote(hid_all.at[ours], hid_all.at[theirs], ctx=across)
    hid_sib = [remote(hid_all.at[at], hid_all.at[at], ctx=sib) for at in (ours, theirs)]
    hid_across.start()
    hid_sib[0].start()

    arrived(sent_y[0])
    paired_y = pair_up(y_rows, y_two)
    back_sum = dot(y_rows[:rows], down_t[...], NN)
    back_move.wait_recv()
    back_sum = back_sum + back_got[...].astype(f32)
    gate, up = pre[0], pre[1]
    sig = 1.0 / (1.0 + jnp.exp(-gate))
    low = lax.rem(me_exp, 2)
    base = core * 2 * rows + rows
    halves = [part(base - rows + at * 2 * cap, 2 * cap) for at in (low, 1 - low)]
    far_halves = [part(base + at * 2 * cap, 2 * cap) for at in (low, 1 - low)]
    d_along = [remote(d_all.at[0, ours], d_all.at[0, theirs], ctx=along)] + [
        remote(d_all.at[1, a], d_all.at[1, b], ctx=along) for a, b in zip(halves, far_halves)
    ]
    d_sib = [
        [remote(d_all.at[m, at], d_all.at[m, at], ctx=sib) for at in (ours, theirs)]
        for m in (0, 1)
    ]
    d_all[0, ours] = (back_sum * up * sig * (1.0 + gate * (1.0 - sig))).astype(bf)
    d_along[0].start()
    d_sib[0][0].start()
    d_all[1, ours] = (back_sum * gate * sig).astype(bf)
    begin(d_along[1:])
    d_sib[1][0].start()

    def slot_rows(to, at):
        back[to] = (
            dot(d_all[0, at], gate_t[...], NN) + dot(d_all[1, at], up_t[...], NN)
        ).astype(bf)

    inner[...] = jnp.broadcast_to(
        jnp.sum(hid_all[ours].astype(f32) * back_sum, axis=1, keepdims=True), inner.shape
    )
    slot_rows(part(0, rows), ours)
    home_own = give_back(back, home, 0, exp_peers, True)
    home_own += give_back(inner, home_inner, 0, exp_peers, True)

    hid_across.wait_recv()
    hid_sib[1].start()
    arrived(paired_x)
    arrived(paired_y)
    d_along[0].wait_recv()
    d_sib[0][1].start()
    arrived(hid_sib)
    down_move = remote(down_send, down_got, ctx=along)
    down_send[...] = dot(hid_all[...], y_two[1 - side_y], TN).astype(bf)
    down_move.start()
    keep_down[...] = dot(hid_all[...], y_two[side_y], TN)
    sum_moves = [remote(sum_send.at[m], sum_got.at[m], ctx=across) for m in (0, 1)]

    def side_sum(m):
        arrived(d_sib[m])
        sum_send[m] = dot(x_two[1 - side_x], d_all[m], TN).astype(bf)
        sum_moves[m].start()
        keep[m] = dot(x_two[side_x], d_all[m], TN)

    side_sum(0)
    d_along[1].wait_recv()
    slot_rows(part(rows + low * 2 * cap, 2 * cap), far_halves[0])
    home_far = give_back(back, home, rows, exp_peers[1:2], True)
    d_along[2].wait_recv()
    d_sib[1][1].start()
    slot_rows(part(rows + (1 - low) * 2 * cap, 2 * cap), far_halves[1])
    home_far += give_back(back, home, rows, exp_peers[::2], False)
    side_sum(1)

    arrived(home_own)
    token_out[:, block] = dot(table[0], home[:rows], TN).astype(bf)
    route_out[...] = (
        jnp.sum(table[0].astype(f32) * home_inner[...], axis=0, keepdims=True) / weight_row[...]
    )
    arrived(home_far)
    tok_move = remote(tok_send, tok_got, ctx=along)
    tok_send[...] = dot(table[1], home[rows:], TN).astype(bf)
    tok_move.start()
    down_move.wait_recv()
    down_grad[...] = (keep_down[...] + down_got[...].astype(f32)).astype(bf)
    for m, out in enumerate((gate_grad, up_grad)):
        sum_moves[m].wait_recv()
        out[...] = (keep[m] + sum_got[m].astype(f32)).astype(bf)
    tok_move.wait_recv()
    token_out[:, other] = tok_got[...]
    copies.sent()


def hand_over(*refs):
    for source, out in zip(refs[:5], refs[5:]):
        out[...] = source[...]


def fast_body(tokens, cotangent, expert_ids, route_weights, w_gate, w_up, w_down):
    n_ctx = lax.axis_size("ctx")
    n_exp = lax.axis_size("exp")
    count, width = tokens.shape
    cap = max(2, (3 * count + 2 * n_exp - 1) // (2 * n_exp))
    cols = width // n_ctx
    units = w_gate.shape[2]
    rows = n_exp * cap
    wide = width // 2
    bf, f32 = jnp.bfloat16, jnp.float32
    vm = pl.BlockSpec(memory_space=pltpu.VMEM)
    hbm = pl.BlockSpec(memory_space=pl.ANY)
    dma = pltpu.SemaphoreType.DMA
    scratch = [
        ((2, count, wide), bf), ((count, width), bf), ((count, width), bf), ((count, wide), bf),
        ((2, 1, count), jnp.int32), ((3, rows, count), bf),
        ((2 * rows, wide), bf), ((2 * rows, wide), bf), ((2 * rows, wide), bf), ((2 * rows, wide), bf),
        ((wide, units), bf), ((wide, units), bf), ((n_ctx // 2, units, cols), bf),
        ((units, wide), bf), ((units, wide), bf), ((wide, units), bf),
        ((2, rows, units), bf), ((2, rows, units), bf), ((2, rows, units), f32),
        ((rows, units), bf), ((rows, units), bf),
        ((4 * rows, units), bf), ((2, 4 * rows, units), bf),
        ((2, 4 * rows, cols), bf), ((2, 4 * rows, cols), bf),
        ((2 * rows, wide), bf), ((2 * rows, wide), bf),
        ((rows, count), f32), ((rows, count), f32),
        ((2, cols, units), f32), ((2, cols, units), bf), ((2, cols, units), bf),
        ((units, cols), f32), ((units, cols), bf), ((units, cols), bf),
        ((count, wide), bf), ((count, wide), bf),
    ]
    token_grads, route, gate_grads, up_grads, down_grads = pl.pallas_call(
        functools.partial(kernel, n_exp, n_ctx, cap),
        out_shape=(
            jax.ShapeDtypeStruct((count, width), bf),
            jax.ShapeDtypeStruct((1, count), f32),
            jax.ShapeDtypeStruct((cols, units), bf),
            jax.ShapeDtypeStruct((cols, units), bf),
            jax.ShapeDtypeStruct((units, cols), bf),
        ),
        in_specs=[hbm] * 2 + [vm] * 2 + [hbm] * 3,
        out_specs=(vm,) * 5,
        scratch_shapes=[pltpu.VMEM(*one) for one in scratch] + [dma((64,)), dma((64,)), dma((40,))],
        compiler_params=pltpu.CompilerParams(
            collective_id=0, has_side_effects=True, vmem_limit_bytes=56 * 1024 * 1024
        ),
    )(
        tokens, cotangent, expert_ids.reshape(1, count), route_weights.reshape(1, count),
        w_gate, w_up, w_down,
    )
    results = (token_grads, route, gate_grads, up_grads, down_grads)
    token_grads, route, gate_grads, up_grads, down_grads = pl.pallas_call(
        hand_over,
        out_shape=tuple(jax.ShapeDtypeStruct(r.shape, r.dtype) for r in results),
        in_specs=[vm] * 5,
        out_specs=(vm,) * 5,
    )(*results)
    return (
        token_grads, route.reshape(count, 1), gate_grads[None], up_grads[None], down_grads[None]
    )


def solution(mesh):
    return jax.shard_map(
        fast_body if (mesh.shape["ctx"], mesh.shape["exp"]) == (8, 4) else body,
        mesh=mesh,
        in_specs=(
            P(("ctx", "exp"), None),
            P(("ctx", "exp"), None),
            P(("ctx", "exp"), None),
            P(("ctx", "exp"), None),
            P("exp", "ctx", None),
            P("exp", "ctx", None),
            P("exp", None, "ctx"),
        ),
        out_specs=(
            P(("ctx", "exp"), None),
            P(("ctx", "exp"), None),
            P("exp", "ctx", None),
            P("exp", "ctx", None),
            P("exp", None, "ctx"),
        ),
        check_vma=False,
    )
```

```python
import functools

import jax
import jax.numpy as jnp
from jax import lax
from jax.experimental import pallas as pl
from jax.experimental.pallas import tpu as pltpu
from jax.sharding import PartitionSpec as P

MESH = pl.DeviceIdType.MESH


def slot_table(route_ids, expert_count, capacity):
    labels = jnp.arange(expert_count, dtype=jnp.int32)
    onehot = (route_ids[..., :, None] == labels).astype(jnp.int32)
    position = jnp.sum((jnp.cumsum(onehot, axis=-2) - 1) * onehot, axis=-1)
    target = route_ids * capacity + position
    places = jnp.arange(expert_count * capacity, dtype=jnp.int32)
    return (target[..., None, :] == places[:, None]).astype(jnp.bfloat16)


def forward_hidden(totals, units):
    gate_pre = totals[:, :units]
    up_pre = totals[:, units:]
    gate_sig = jax.nn.sigmoid(gate_pre)
    return (gate_pre * gate_sig * up_pre).astype(jnp.bfloat16)


def backward_grads(totals, back_sum, units):
    gate_pre = totals[:, :units]
    up_pre = totals[:, units:]
    gate_sig = jax.nn.sigmoid(gate_pre)
    d_up = (back_sum * gate_pre * gate_sig).astype(jnp.bfloat16)
    d_gate = (back_sum * up_pre * gate_sig * (1.0 + gate_pre * (1.0 - gate_sig))).astype(
        jnp.bfloat16
    )
    return jnp.concatenate([d_gate, d_up], axis=1)


def body(tokens, cotangent, expert_ids, route_weights, w_gate, w_up, w_down):
    ctx_size = lax.axis_size("ctx")
    exp_size = lax.axis_size("exp")
    tok_count, model_width = tokens.shape
    route_count = expert_ids.shape[1]
    slot_count = tok_count * route_count
    expert_count = w_gate.shape[0] * exp_size
    capacity = max(2, (3 * slot_count + 2 * expert_count - 1) // (2 * expert_count))
    col_count = model_width // ctx_size
    units = w_gate.shape[2]
    row_count = ctx_size * exp_size * capacity
    own_rows = row_count // ctx_size
    all_ids = lax.all_gather(expert_ids, "ctx", axis=0, tiled=True)
    tables = slot_table(all_ids.reshape(ctx_size, slot_count), expert_count, capacity)
    token_slots = jnp.repeat(tokens, route_count, axis=0)
    scaled = (
        route_weights * jnp.repeat(cotangent, route_count, axis=0).astype(jnp.float32)
    ).astype(jnp.bfloat16)
    own_table = lax.dynamic_index_in_dim(tables, lax.axis_index("ctx"), 0, keepdims=False)
    send_x = jnp.dot(own_table, token_slots, preferred_element_type=jnp.float32).astype(
        jnp.bfloat16
    )
    send_y = jnp.dot(own_table, scaled, preferred_element_type=jnp.float32).astype(jnp.bfloat16)
    send_x = send_x.reshape(expert_count, capacity, model_width)
    send_y = send_y.reshape(expert_count, capacity, model_width)
    group_x, group_y = (
        lax.all_to_all(send_x, "exp", split_axis=0, concat_axis=0, tiled=True),
        lax.all_to_all(send_y, "exp", split_axis=0, concat_axis=0, tiled=True),
    )
    slot_x, slot_y = (
        lax.all_to_all(group_x, "ctx", split_axis=2, concat_axis=0, tiled=True),
        lax.all_to_all(group_y, "ctx", split_axis=2, concat_axis=0, tiled=True),
    )
    slot_x = slot_x.reshape(row_count, col_count)
    slot_y = slot_y.reshape(row_count, col_count)
    gate_weight = w_gate[0]
    up_weight = w_up[0]
    down_weight = w_down[0]
    both_weights = jnp.concatenate([gate_weight, up_weight], axis=1)

    def fold_grad(segment):
        gate_acc = lax.dot_general(
            slot_x, segment[:, :units], (((0,), (0,)), ((), ())), preferred_element_type=jnp.float32
        )
        up_acc = lax.dot_general(
            slot_x, segment[:, units:], (((0,), (0,)), ((), ())), preferred_element_type=jnp.float32
        )
        grad_rows = lax.dot_general(
            segment, both_weights, (((1,), (1,)), ((), ())), preferred_element_type=jnp.float32
        )
        return (gate_acc, up_acc, grad_rows)

    row_x, row_y = (
        lax.all_to_all(slot_x, "ctx", split_axis=0, concat_axis=1, tiled=True),
        lax.all_to_all(slot_y, "ctx", split_axis=0, concat_axis=1, tiled=True),
    )
    full_gate, full_up, full_down = (
        lax.all_gather(gate_weight, "ctx", axis=0, tiled=True),
        lax.all_gather(up_weight, "ctx", axis=0, tiled=True),
        lax.all_gather(down_weight, "ctx", axis=1, tiled=True),
    )
    full_both = jnp.concatenate([full_gate, full_up], axis=1).reshape(
        ctx_size, col_count, 2 * units
    )
    gate_blocks = jnp.einsum(
        "rcd,cdf->crf",
        row_x.reshape(own_rows, ctx_size, col_count),
        full_both,
        preferred_element_type=jnp.float32,
    ).astype(jnp.bfloat16)
    totals_own = jnp.sum(gate_blocks.astype(jnp.float32), axis=0)
    hidden_own = forward_hidden(totals_own, units)
    back_blocks = jnp.einsum(
        "rcd,fcd->crf",
        row_y.reshape(own_rows, ctx_size, col_count),
        full_down.reshape(units, ctx_size, col_count),
        preferred_element_type=jnp.float32,
    ).astype(jnp.bfloat16)
    back_own = jnp.sum(back_blocks.astype(jnp.float32), axis=0)
    grads_own = backward_grads(totals_own, back_own, units)
    segment = (
        lax.all_gather(hidden_own, "ctx", axis=0, tiled=True),
        lax.all_gather(grads_own, "ctx", axis=0, tiled=True),
    )
    fold_segment = segment[0]
    outputs = jnp.dot(fold_segment, down_weight, preferred_element_type=jnp.float32)
    inner_rows = jnp.sum(slot_y.astype(jnp.float32) * outputs, axis=1)
    inner_all = inner_rows
    down_acc = lax.dot_general(
        fold_segment, slot_y, (((0,), (0,)), ((), ())), preferred_element_type=jnp.float32
    )
    down_state = (down_acc, inner_all)
    grad_state = fold_grad(segment[1])
    down_acc = down_state[0]
    inner_all = down_state[1]
    gate_acc = grad_state[0]
    up_acc = grad_state[1]
    back_rows = grad_state[2]
    back_slots = back_rows.astype(jnp.bfloat16).reshape(ctx_size, exp_size, capacity, col_count)
    inner_slots = inner_all.reshape(ctx_size, exp_size, capacity)
    home_back = lax.all_to_all(back_slots, "exp", split_axis=1, concat_axis=1, tiled=True)
    home_inner = lax.all_to_all(inner_slots, "exp", split_axis=1, concat_axis=1, tiled=True)
    merged = jnp.einsum(
        "cks,ckd->csd",
        tables,
        home_back.reshape(ctx_size, expert_count * capacity, col_count),
        preferred_element_type=jnp.float32,
    )
    merged = jnp.sum(merged.reshape(ctx_size, tok_count, route_count, col_count), axis=2).astype(
        jnp.bfloat16
    )
    grads_home = lax.all_to_all(merged, "ctx", split_axis=0, concat_axis=2, tiled=True)
    token_grads = grads_home.reshape(tok_count, model_width)
    inner_home = jnp.einsum(
        "cks,ck->cs",
        tables.astype(jnp.float32),
        home_inner.reshape(ctx_size, expert_count * capacity),
        precision=lax.Precision.HIGHEST,
    )
    route_sums = lax.psum_scatter(inner_home, "ctx", scatter_dimension=0, tiled=True).reshape(
        tok_count, route_count
    )
    route_grads = route_sums / route_weights
    gate_grads = gate_acc.astype(jnp.bfloat16)[None]
    up_grads = up_acc.astype(jnp.bfloat16)[None]
    down_grads = down_acc.astype(jnp.bfloat16)[None]
    return (token_grads, route_grads, gate_grads, up_grads, down_grads)


def ctx_neighbours(me):
    sib = me + 1 - 2 * (me % 2)
    across = me + 2 - 4 * ((me // 2) % 2)
    along = me + 4 - 8 * ((me // 4) % 2)
    return sib, across, along


def greet(ctx_peers, exp_peers):
    barrier = pltpu.get_barrier_semaphore()
    for peer in ctx_peers:
        pl.semaphore_signal(barrier, inc=1, device_id={"ctx": peer}, device_id_type=MESH)
    for peer in exp_peers:
        pl.semaphore_signal(barrier, inc=1, device_id={"exp": peer}, device_id_type=MESH)
    return len(ctx_peers) + len(exp_peers)


class Copies:
    def __init__(self, send_sem, recv_sem, local_sem):
        self.sems = send_sem, recv_sem, local_sem
        self.far, self.near = [], 0

    def remote(self, source, target, **peer):
        k = len(self.far)
        one = pltpu.make_async_remote_copy(
            src_ref=source,
            dst_ref=target,
            send_sem=self.sems[0].at[k],
            recv_sem=self.sems[1].at[k],
            device_id=peer,
            device_id_type=MESH,
        )
        self.far.append(one)
        return one

    def local(self, source, target):
        one = pltpu.make_async_copy(source, target, self.sems[2].at[self.near])
        self.near += 1
        return one

    def sent(self):
        for one in self.far:
            one.wait_send()


def begin(copies):
    for one in copies:
        one.start()


def arrived(copies):
    for one in copies:
        one.wait_recv()


NT = (((1,), (1,)), ((), ()))
TN = (((0,), (0,)), ((), ()))
NN = (((1,), (0,)), ((), ()))


def dot(a, b, dims):
    return lax.dot_general(a, b, dims, preferred_element_type=jnp.float32)


def kernel(
    n_exp, n_ctx, cap,
    tok_in, cot_in, ids_row, weight_row, w_gate, w_up, w_down,
    token_out, route_out, gate_grad, up_grad, down_grad,
    tok, cot, scaled, scaled_far, ids_far, table, send_x, x_rows, send_y, y_rows,
    gate_w, up_w, down_w, gate_t, up_t, down_t,
    pre_send, pre_got, pre, back_send, back_got, hid_all, d_all, x_two, y_two,
    back, home, inner, home_inner,
    keep, sum_send, sum_got, keep_down, down_send, down_got, tok_send, tok_got,
    send_sem, recv_sem, local_sem,
):
    me_exp = lax.axis_index("exp")
    me = lax.axis_index("ctx")
    bf, f32 = jnp.bfloat16, jnp.float32
    sib, across, along = ctx_neighbours(me)
    core = lax.rem(me, 2)
    side_x = lax.rem(lax.div(me, 2), 2)
    side_y = lax.div(me, 4)
    exp_peers = [lax.rem(me_exp + d, n_exp) for d in range(1, n_exp)]
    count, width = cot.shape
    cols = width // n_ctx
    rows = n_exp * cap
    wide, strip = width // 2, width // 4

    def cut(at, size):
        return pl.ds(pl.multiple_of(at * size, size), size)

    def part(base, size):
        return pl.ds(pl.multiple_of(base, 16), size)

    copies = Copies(send_sem, recv_sem, local_sem)
    remote, local = copies.remote, copies.local
    block, other = cut(side_y, wide), cut(1 - side_y, wide)
    loads = [local(cot_in, cot), local(tok_in.at[:, block], tok.at[0])]
    begin(loads)
    greeted = greet([sib, across, along], exp_peers)

    down_i = lax.broadcasted_iota(jnp.int32, (count, count), 0)
    over_i = lax.broadcasted_iota(jnp.int32, (count, count), 1)
    diagonal = down_i == over_i

    def fill_table(at, row):
        row_f = row.astype(f32)
        col_f = jnp.sum(jnp.where(diagonal, row_f, 0.0), axis=1, keepdims=True)
        position = jnp.sum(
            jnp.where((col_f == row_f) & (down_i < over_i), 1.0, 0.0), axis=0, keepdims=True
        )
        target = row * cap + position.astype(jnp.int32)
        places = lax.broadcasted_iota(jnp.int32, (rows, count), 0)
        table[at] = jnp.where(places == target, 1.0, 0.0).astype(bf)

    def place(at):
        return (lax.rem(at, 2) * 2 + lax.div(at, 2)) * cap

    def scatter(source, out, base):
        moves = [
            remote(
                source.at[part(base + peer * cap, cap)],
                out.at[part(base + place(me_exp), cap)],
                exp=peer,
            )
            for peer in exp_peers
        ]
        moves.append(
            local(
                source.at[part(base + me_exp * cap, cap)],
                out.at[part(base + place(me_exp), cap)],
            )
        )
        return moves

    def give_back(source, out, base, peers, own):
        moves = [
            remote(
                source.at[part(base + place(peer), cap)],
                out.at[part(base + me_exp * cap, cap)],
                exp=peer,
            )
            for peer in peers
        ]
        if own:
            moves.append(
                local(
                    source.at[part(base + place(me_exp), cap)],
                    out.at[part(base + me_exp * cap, cap)],
                )
            )
        begin(moves)
        return moves

    fill_table(0, ids_row[...])
    weight_col = jnp.sum(jnp.where(diagonal, weight_row[...], 0.0), axis=1, keepdims=True)
    loads[0].wait()
    scaled[...] = (weight_col * cot[...].astype(f32)).astype(bf)
    loads[1].wait()
    send_x[:rows] = dot(table[0], tok[0], NN).astype(bf)

    def gathered(own, out, at, at_peer, peer):
        return (
            remote(own.at[0], out.at[at], ctx=peer),
            remote(own.at[0], out.at[at], ctx=sib),
            remote(out.at[at_peer], out.at[at_peer], ctx=sib),
            local(own.at[0], out.at[at]),
        )

    at, at_across = cut(lax.rem(me, 4), cols), cut(lax.rem(across, 4), cols)
    side_w = [gathered(own, out, at, at_across, across) for own, out in ((w_gate, gate_w), (w_up, up_w))]
    side_w.append(gathered(w_down, down_w, side_y * 2 + core, (1 - side_y) * 2 + core, along))
    spread_x = [
        remote(ids_row, ids_far.at[0], ctx=along),
        remote(tok_in.at[:, other], tok.at[1], ctx=along),
    ]
    spread_y = [remote(ids_row, ids_far.at[1], ctx=across)] + [
        remote(
            scaled.at[:, cut(2 * s + 1 - side_x, strip)],
            scaled_far.at[:, s * strip:(s + 1) * strip],
            ctx=across,
        )
        for s in range(2)
    ]
    sent_x = [scatter(send_x, x_rows, base) for base in (0, rows)]
    sent_y = [scatter(send_y, y_rows, base) for base in (0, rows)]
    pl.semaphore_wait(pltpu.get_barrier_semaphore(), greeted)
    begin(spread_x)
    begin(spread_y)
    begin(sent_x[0])
    for g in side_w:
        g[0].start()
    for s in range(2):
        send_y[:rows, s * strip:(s + 1) * strip] = dot(
            table[0], scaled[:, cut(2 * s + side_x, strip)], NN
        ).astype(bf)
    spread_x[0].wait_recv()
    fill_table(1, ids_far[0])
    spread_x[1].wait_recv()
    send_x[rows:] = dot(table[1], tok[1], NN).astype(bf)
    begin(sent_x[1])
    for g in side_w:
        begin(g[1::2])
    spread_y[0].wait_recv()
    fill_table(2, ids_far[1])
    arrived(spread_y[1:])
    send_y[rows:] = dot(table[2], scaled_far[...], NN).astype(bf)

    def all_here(g):
        g[3].wait()
        g[1].wait_recv()
        g[2].wait_recv()

    def pass_on(g):
        g[0].wait_recv()
        g[2].start()

    pre_moves = [remote(pre_send.at[m], pre_got.at[m], ctx=along) for m in (0, 1)]
    pass_on(side_w[0])
    begin(sent_y[1])
    begin(sent_y[0])
    pass_on(side_w[2])
    arrived(sent_x[0])
    all_here(side_w[0])
    pre[0] = dot(x_rows[:rows], gate_w[...], NN)
    arrived(sent_x[1])
    pre_send[0] = dot(x_rows[rows:], gate_w[...], NN).astype(bf)
    pre_moves[0].start()
    pair = cut(core, 2 * rows)

    def pair_up(source, out):
        moves = []
        for q in range(2):
            moves.append(
                remote(source.at[:, cut(2 * q + 1 - core, cols)], out.at[q, pair], ctx=sib)
            )
            moves.append(local(source.at[:, cut(2 * q + core, cols)], out.at[q, pair]))
        begin(moves)
        return moves

    paired_x = pair_up(x_rows, x_two)
    all_here(side_w[2])
    for q in range(4):
        down_t[q * cols:(q + 1) * cols] = down_w[q].T
    pass_on(side_w[1])
    all_here(side_w[1])
    pre_send[1] = dot(x_rows[rows:], up_w[...], NN).astype(bf)
    pre_moves[1].start()
    pre[1] = dot(x_rows[:rows], up_w[...], NN)
    back_move = remote(back_send, back_got, ctx=across)
    arrived(sent_y[1])
    back_send[...] = dot(y_rows[rows:], down_t[...], NN).astype(bf)
    back_move.start()
    gate_t[...] = gate_w[...].T
    up_t[...] = up_w[...].T

    ours = part(core * 2 * rows, rows)
    theirs = part(core * 2 * rows + rows, rows)
    pre_moves[0].wait_recv()
    pre[0] = pre[0] + pre_got[0].astype(f32)
    pre_moves[1].wait_recv()
    pre[1] = pre[1] + pre_got[1].astype(f32)
    gate, up = pre[0], pre[1]
    sig = 1.0 / (1.0 + jnp.exp(-gate))
    hidden = (gate * sig * up).astype(bf)
    hid_all[ours] = hidden
    hid_across = remote(hid_all.at[ours], hid_all.at[theirs], ctx=across)
    hid_sib = [remote(hid_all.at[at], hid_all.at[at], ctx=sib) for at in (ours, theirs)]
    hid_across.start()
    hid_sib[0].start()

    arrived(sent_y[0])
    paired_y = pair_up(y_rows, y_two)
    back_sum = dot(y_rows[:rows], down_t[...], NN)
    back_move.wait_recv()
    back_sum = back_sum + back_got[...].astype(f32)
    gate, up = pre[0], pre[1]
    sig = 1.0 / (1.0 + jnp.exp(-gate))
    low = lax.rem(me_exp, 2)
    base = core * 2 * rows + rows
    halves = [part(base - rows + at * 2 * cap, 2 * cap) for at in (low, 1 - low)]
    far_halves = [part(base + at * 2 * cap, 2 * cap) for at in (low, 1 - low)]
    d_along = [remote(d_all.at[0, ours], d_all.at[0, theirs], ctx=along)] + [
        remote(d_all.at[1, a], d_all.at[1, b], ctx=along) for a, b in zip(halves, far_halves)
    ]
    d_sib = [
        [remote(d_all.at[m, at], d_all.at[m, at], ctx=sib) for at in (ours, theirs)]
        for m in (0, 1)
    ]
    d_all[0, ours] = (back_sum * up * sig * (1.0 + gate * (1.0 - sig))).astype(bf)
    d_along[0].start()
    d_sib[0][0].start()
    d_all[1, ours] = (back_sum * gate * sig).astype(bf)
    begin(d_along[1:])
    d_sib[1][0].start()

    def slot_rows(to, at):
        back[to] = (
            dot(d_all[0, at], gate_t[...], NN) + dot(d_all[1, at], up_t[...], NN)
        ).astype(bf)

    inner[...] = jnp.broadcast_to(
        jnp.sum(hid_all[ours].astype(f32) * back_sum, axis=1, keepdims=True), inner.shape
    )
    slot_rows(part(0, rows), ours)
    home_own = give_back(back, home, 0, exp_peers, True)
    home_own += give_back(inner, home_inner, 0, exp_peers, True)

    hid_across.wait_recv()
    hid_sib[1].start()
    arrived(paired_x)
    arrived(paired_y)
    d_along[0].wait_recv()
    d_sib[0][1].start()
    arrived(hid_sib)
    down_move = remote(down_send, down_got, ctx=along)
    down_send[...] = dot(hid_all[...], y_two[1 - side_y], TN).astype(bf)
    down_move.start()
    keep_down[...] = dot(hid_all[...], y_two[side_y], TN)
    sum_moves = [remote(sum_send.at[m], sum_got.at[m], ctx=across) for m in (0, 1)]

    def side_sum(m):
        arrived(d_sib[m])
        sum_send[m] = dot(x_two[1 - side_x], d_all[m], TN).astype(bf)
        sum_moves[m].start()
        keep[m] = dot(x_two[side_x], d_all[m], TN)

    side_sum(0)
    d_along[1].wait_recv()
    slot_rows(part(rows + low * 2 * cap, 2 * cap), far_halves[0])
    home_far = give_back(back, home, rows, exp_peers[1:2], True)
    d_along[2].wait_recv()
    d_sib[1][1].start()
    slot_rows(part(rows + (1 - low) * 2 * cap, 2 * cap), far_halves[1])
    home_far += give_back(back, home, rows, exp_peers[::2], False)
    side_sum(1)

    arrived(home_own)
    token_out[:, block] = dot(table[0], home[:rows], TN).astype(bf)
    route_out[...] = (
        jnp.sum(table[0].astype(f32) * home_inner[...], axis=0, keepdims=True) / weight_row[...]
    )
    arrived(home_far)
    tok_move = remote(tok_send, tok_got, ctx=along)
    tok_send[...] = dot(table[1], home[rows:], TN).astype(bf)
    tok_move.start()
    down_move.wait_recv()
    down_grad[...] = (keep_down[...] + down_got[...].astype(f32)).astype(bf)
    for m, out in enumerate((gate_grad, up_grad)):
        sum_moves[m].wait_recv()
        out[...] = (keep[m] + sum_got[m].astype(f32)).astype(bf)
    tok_move.wait_recv()
    token_out[:, other] = tok_got[...]
    copies.sent()


def hand_over(*refs):
    for source, out in zip(refs[:5], refs[5:]):
        out[...] = source[...]


def fast_body(tokens, cotangent, expert_ids, route_weights, w_gate, w_up, w_down):
    n_ctx = lax.axis_size("ctx")
    n_exp = lax.axis_size("exp")
    count, width = tokens.shape
    cap = max(2, (3 * count + 2 * n_exp - 1) // (2 * n_exp))
    cols = width // n_ctx
    units = w_gate.shape[2]
    rows = n_exp * cap
    wide = width // 2
    bf, f32 = jnp.bfloat16, jnp.float32
    vm = pl.BlockSpec(memory_space=pltpu.VMEM)
    hbm = pl.BlockSpec(memory_space=pl.ANY)
    dma = pltpu.SemaphoreType.DMA
    scratch = [
        ((2, count, wide), bf), ((count, width), bf), ((count, width), bf), ((count, wide), bf),
        ((2, 1, count), jnp.int32), ((3, rows, count), bf),
        ((2 * rows, wide), bf), ((2 * rows, wide), bf), ((2 * rows, wide), bf), ((2 * rows, wide), bf),
        ((wide, units), bf), ((wide, units), bf), ((n_ctx // 2, units, cols), bf),
        ((units, wide), bf), ((units, wide), bf), ((wide, units), bf),
        ((2, rows, units), bf), ((2, rows, units), bf), ((2, rows, units), f32),
        ((rows, units), bf), ((rows, units), bf),
        ((4 * rows, units), bf), ((2, 4 * rows, units), bf),
        ((2, 4 * rows, cols), bf), ((2, 4 * rows, cols), bf),
        ((2 * rows, wide), bf), ((2 * rows, wide), bf),
        ((rows, count), f32), ((rows, count), f32),
        ((2, cols, units), f32), ((2, cols, units), bf), ((2, cols, units), bf),
        ((units, cols), f32), ((units, cols), bf), ((units, cols), bf),
        ((count, wide), bf), ((count, wide), bf),
    ]
    token_grads, route, gate_grads, up_grads, down_grads = pl.pallas_call(
        functools.partial(kernel, n_exp, n_ctx, cap),
        out_shape=(
            jax.ShapeDtypeStruct((count, width), bf),
            jax.ShapeDtypeStruct((1, count), f32),
            jax.ShapeDtypeStruct((cols, units), bf),
            jax.ShapeDtypeStruct((cols, units), bf),
            jax.ShapeDtypeStruct((units, cols), bf),
        ),
        in_specs=[hbm] * 2 + [vm] * 2 + [hbm] * 3,
        out_specs=(vm,) * 5,
        scratch_shapes=[pltpu.VMEM(*one) for one in scratch] + [dma((64,)), dma((64,)), dma((40,))],
        compiler_params=pltpu.CompilerParams(
            collective_id=0, has_side_effects=True, vmem_limit_bytes=56 * 1024 * 1024
        ),
    )(
        tokens, cotangent, expert_ids.reshape(1, count), route_weights.reshape(1, count),
        w_gate, w_up, w_down,
    )
    results = (token_grads, route, gate_grads, up_grads, down_grads)
    token_grads, route, gate_grads, up_grads, down_grads = pl.pallas_call(
        hand_over,
        out_shape=tuple(jax.ShapeDtypeStruct(r.shape, r.dtype) for r in results),
        in_specs=[vm] * 5,
        out_specs=(vm,) * 5,
    )(*results)
    return (
        token_grads, route.reshape(count, 1), gate_grads[None], up_grads[None], down_grads[None]
    )


def solution(mesh):
    return jax.shard_map(
        fast_body if (mesh.shape["ctx"], mesh.shape["exp"]) == (8, 4) else body,
        mesh=mesh,
        in_specs=(
            P(("ctx", "exp"), None),
            P(("ctx", "exp"), None),
            P(("ctx", "exp"), None),
            P(("ctx", "exp"), None),
            P("exp", "ctx", None),
            P("exp", "ctx", None),
            P("exp", None, "ctx"),
        ),
        out_specs=(
            P(("ctx", "exp"), None),
            P(("ctx", "exp"), None),
            P("exp", "ctx", None),
            P("exp", "ctx", None),
            P("exp", None, "ctx"),
        ),
        check_vma=False,
    )
```

```python
import functools

import jax
import jax.numpy as jnp
from jax import lax
from jax.experimental import pallas as pl
from jax.experimental.pallas import tpu as pltpu
from jax.sharding import PartitionSpec as P

MESH = pl.DeviceIdType.MESH


def slot_table(route_ids, expert_count, capacity):
    labels = jnp.arange(expert_count, dtype=jnp.int32)
    onehot = (route_ids[..., :, None] == labels).astype(jnp.int32)
    position = jnp.sum((jnp.cumsum(onehot, axis=-2) - 1) * onehot, axis=-1)
    target = route_ids * capacity + position
    places = jnp.arange(expert_count * capacity, dtype=jnp.int32)
    return (target[..., None, :] == places[:, None]).astype(jnp.bfloat16)


def forward_hidden(totals, units):
    gate_pre = totals[:, :units]
    up_pre = totals[:, units:]
    gate_sig = jax.nn.sigmoid(gate_pre)
    return (gate_pre * gate_sig * up_pre).astype(jnp.bfloat16)


def backward_grads(totals, back_sum, units):
    gate_pre = totals[:, :units]
    up_pre = totals[:, units:]
    gate_sig = jax.nn.sigmoid(gate_pre)
    d_up = (back_sum * gate_pre * gate_sig).astype(jnp.bfloat16)
    d_gate = (back_sum * up_pre * gate_sig * (1.0 + gate_pre * (1.0 - gate_sig))).astype(
        jnp.bfloat16
    )
    return jnp.concatenate([d_gate, d_up], axis=1)


def body(tokens, cotangent, expert_ids, route_weights, w_gate, w_up, w_down):
    ctx_size = lax.axis_size("ctx")
    exp_size = lax.axis_size("exp")
    tok_count, model_width = tokens.shape
    route_count = expert_ids.shape[1]
    slot_count = tok_count * route_count
    expert_count = w_gate.shape[0] * exp_size
    capacity = max(2, (3 * slot_count + 2 * expert_count - 1) // (2 * expert_count))
    col_count = model_width // ctx_size
    units = w_gate.shape[2]
    row_count = ctx_size * exp_size * capacity
    own_rows = row_count // ctx_size
    all_ids = lax.all_gather(expert_ids, "ctx", axis=0, tiled=True)
    tables = slot_table(all_ids.reshape(ctx_size, slot_count), expert_count, capacity)
    token_slots = jnp.repeat(tokens, route_count, axis=0)
    scaled = (
        route_weights * jnp.repeat(cotangent, route_count, axis=0).astype(jnp.float32)
    ).astype(jnp.bfloat16)
    own_table = lax.dynamic_index_in_dim(tables, lax.axis_index("ctx"), 0, keepdims=False)
    send_x = jnp.dot(own_table, token_slots, preferred_element_type=jnp.float32).astype(
        jnp.bfloat16
    )
    send_y = jnp.dot(own_table, scaled, preferred_element_type=jnp.float32).astype(jnp.bfloat16)
    send_x = send_x.reshape(expert_count, capacity, model_width)
    send_y = send_y.reshape(expert_count, capacity, model_width)
    group_x, group_y = (
        lax.all_to_all(send_x, "exp", split_axis=0, concat_axis=0, tiled=True),
        lax.all_to_all(send_y, "exp", split_axis=0, concat_axis=0, tiled=True),
    )
    slot_x, slot_y = (
        lax.all_to_all(group_x, "ctx", split_axis=2, concat_axis=0, tiled=True),
        lax.all_to_all(group_y, "ctx", split_axis=2, concat_axis=0, tiled=True),
    )
    slot_x = slot_x.reshape(row_count, col_count)
    slot_y = slot_y.reshape(row_count, col_count)
    gate_weight = w_gate[0]
    up_weight = w_up[0]
    down_weight = w_down[0]
    both_weights = jnp.concatenate([gate_weight, up_weight], axis=1)

    def fold_grad(segment):
        gate_acc = lax.dot_general(
            slot_x, segment[:, :units], (((0,), (0,)), ((), ())), preferred_element_type=jnp.float32
        )
        up_acc = lax.dot_general(
            slot_x, segment[:, units:], (((0,), (0,)), ((), ())), preferred_element_type=jnp.float32
        )
        grad_rows = lax.dot_general(
            segment, both_weights, (((1,), (1,)), ((), ())), preferred_element_type=jnp.float32
        )
        return (gate_acc, up_acc, grad_rows)

    row_x, row_y = (
        lax.all_to_all(slot_x, "ctx", split_axis=0, concat_axis=1, tiled=True),
        lax.all_to_all(slot_y, "ctx", split_axis=0, concat_axis=1, tiled=True),
    )
    full_gate, full_up, full_down = (
        lax.all_gather(gate_weight, "ctx", axis=0, tiled=True),
        lax.all_gather(up_weight, "ctx", axis=0, tiled=True),
        lax.all_gather(down_weight, "ctx", axis=1, tiled=True),
    )
    full_both = jnp.concatenate([full_gate, full_up], axis=1).reshape(
        ctx_size, col_count, 2 * units
    )
    gate_blocks = jnp.einsum(
        "rcd,cdf->crf",
        row_x.reshape(own_rows, ctx_size, col_count),
        full_both,
        preferred_element_type=jnp.float32,
    ).astype(jnp.bfloat16)
    totals_own = jnp.sum(gate_blocks.astype(jnp.float32), axis=0)
    hidden_own = forward_hidden(totals_own, units)
    back_blocks = jnp.einsum(
        "rcd,fcd->crf",
        row_y.reshape(own_rows, ctx_size, col_count),
        full_down.reshape(units, ctx_size, col_count),
        preferred_element_type=jnp.float32,
    ).astype(jnp.bfloat16)
    back_own = jnp.sum(back_blocks.astype(jnp.float32), axis=0)
    grads_own = backward_grads(totals_own, back_own, units)
    segment = (
        lax.all_gather(hidden_own, "ctx", axis=0, tiled=True),
        lax.all_gather(grads_own, "ctx", axis=0, tiled=True),
    )
    fold_segment = segment[0]
    outputs = jnp.dot(fold_segment, down_weight, preferred_element_type=jnp.float32)
    inner_rows = jnp.sum(slot_y.astype(jnp.float32) * outputs, axis=1)
    inner_all = inner_rows
    down_acc = lax.dot_general(
        fold_segment, slot_y, (((0,), (0,)), ((), ())), preferred_element_type=jnp.float32
    )
    down_state = (down_acc, inner_all)
    grad_state = fold_grad(segment[1])
    down_acc = down_state[0]
    inner_all = down_state[1]
    gate_acc = grad_state[0]
    up_acc = grad_state[1]
    back_rows = grad_state[2]
    back_slots = back_rows.astype(jnp.bfloat16).reshape(ctx_size, exp_size, capacity, col_count)
    inner_slots = inner_all.reshape(ctx_size, exp_size, capacity)
    home_back = lax.all_to_all(back_slots, "exp", split_axis=1, concat_axis=1, tiled=True)
    home_inner = lax.all_to_all(inner_slots, "exp", split_axis=1, concat_axis=1, tiled=True)
    merged = jnp.einsum(
        "cks,ckd->csd",
        tables,
        home_back.reshape(ctx_size, expert_count * capacity, col_count),
        preferred_element_type=jnp.float32,
    )
    merged = jnp.sum(merged.reshape(ctx_size, tok_count, route_count, col_count), axis=2).astype(
        jnp.bfloat16
    )
    grads_home = lax.all_to_all(merged, "ctx", split_axis=0, concat_axis=2, tiled=True)
    token_grads = grads_home.reshape(tok_count, model_width)
    inner_home = jnp.einsum(
        "cks,ck->cs",
        tables.astype(jnp.float32),
        home_inner.reshape(ctx_size, expert_count * capacity),
        precision=lax.Precision.HIGHEST,
    )
    route_sums = lax.psum_scatter(inner_home, "ctx", scatter_dimension=0, tiled=True).reshape(
        tok_count, route_count
    )
    route_grads = route_sums / route_weights
    gate_grads = gate_acc.astype(jnp.bfloat16)[None]
    up_grads = up_acc.astype(jnp.bfloat16)[None]
    down_grads = down_acc.astype(jnp.bfloat16)[None]
    return (token_grads, route_grads, gate_grads, up_grads, down_grads)


def ctx_neighbours(me):
    sib = me + 1 - 2 * (me % 2)
    across = me + 2 - 4 * ((me // 2) % 2)
    along = me + 4 - 8 * ((me // 4) % 2)
    return sib, across, along


def greet(ctx_peers, exp_peers):
    barrier = pltpu.get_barrier_semaphore()
    for peer in ctx_peers:
        pl.semaphore_signal(barrier, inc=1, device_id={"ctx": peer}, device_id_type=MESH)
    for peer in exp_peers:
        pl.semaphore_signal(barrier, inc=1, device_id={"exp": peer}, device_id_type=MESH)
    return len(ctx_peers) + len(exp_peers)


class Copies:
    def __init__(self, send_sem, recv_sem, local_sem):
        self.sems = send_sem, recv_sem, local_sem
        self.far, self.near = [], 0

    def remote(self, source, target, **peer):
        k = len(self.far)
        one = pltpu.make_async_remote_copy(
            src_ref=source,
            dst_ref=target,
            send_sem=self.sems[0].at[k],
            recv_sem=self.sems[1].at[k],
            device_id=peer,
            device_id_type=MESH,
        )
        self.far.append(one)
        return one

    def local(self, source, target):
        one = pltpu.make_async_copy(source, target, self.sems[2].at[self.near])
        self.near += 1
        return one

    def sent(self):
        for one in self.far:
            one.wait_send()


def begin(copies):
    for one in copies:
        one.start()


def arrived(copies):
    for one in copies:
        one.wait_recv()


NT = (((1,), (1,)), ((), ()))
TN = (((0,), (0,)), ((), ()))
NN = (((1,), (0,)), ((), ()))


def dot(a, b, dims):
    return lax.dot_general(a, b, dims, preferred_element_type=jnp.float32)


def kernel(
    n_exp, n_ctx, cap,
    tok_in, cot_in, ids_row, weight_row, w_gate, w_up, w_down,
    token_out, route_out, gate_grad, up_grad, down_grad,
    tok, cot, scaled, scaled_far, ids_far, table, send_x, x_rows, send_y, y_rows,
    gate_w, up_w, down_w, gate_t, up_t, down_t,
    pre_send, pre_got, pre, slope, back_send, back_got, hid_all, d_all, x_two, y_two,
    back, home, inner, home_inner,
    keep, sum_send, sum_got, keep_down, down_send, down_got, tok_send, tok_got,
    send_sem, recv_sem, local_sem,
):
    me_exp = lax.axis_index("exp")
    me = lax.axis_index("ctx")
    bf, f32 = jnp.bfloat16, jnp.float32
    sib, across, along = ctx_neighbours(me)
    core = lax.rem(me, 2)
    side_x = lax.rem(lax.div(me, 2), 2)
    side_y = lax.div(me, 4)
    exp_peers = [lax.rem(me_exp + d, n_exp) for d in range(1, n_exp)]
    count, width = cot.shape
    cols = width // n_ctx
    rows = n_exp * cap
    wide, strip = width // 2, width // 4

    def cut(at, size):
        return pl.ds(pl.multiple_of(at * size, size), size)

    def part(base, size):
        return pl.ds(pl.multiple_of(base, 16), size)

    copies = Copies(send_sem, recv_sem, local_sem)
    remote, local = copies.remote, copies.local
    block, other = cut(side_y, wide), cut(1 - side_y, wide)
    loads = [local(cot_in, cot), local(tok_in.at[:, block], tok.at[0])]
    begin(loads)
    greeted = greet([sib, across, along], exp_peers)

    down_i = lax.broadcasted_iota(jnp.int32, (count, count), 0)
    over_i = lax.broadcasted_iota(jnp.int32, (count, count), 1)
    diagonal = down_i == over_i

    def fill_table(at, row):
        row_f = row.astype(f32)
        col_f = jnp.sum(jnp.where(diagonal, row_f, 0.0), axis=1, keepdims=True)
        position = jnp.sum(
            jnp.where((col_f == row_f) & (down_i < over_i), 1.0, 0.0), axis=0, keepdims=True
        )
        target = row * cap + position.astype(jnp.int32)
        places = lax.broadcasted_iota(jnp.int32, (rows, count), 0)
        table[at] = jnp.where(places == target, 1.0, 0.0).astype(bf)

    def place(at):
        return (lax.rem(at, 2) * 2 + lax.div(at, 2)) * cap

    def scatter(source, out, base):
        moves = [
            remote(
                source.at[part(base + peer * cap, cap)],
                out.at[part(base + place(me_exp), cap)],
                exp=peer,
            )
            for peer in exp_peers
        ]
        moves.append(
            local(
                source.at[part(base + me_exp * cap, cap)],
                out.at[part(base + place(me_exp), cap)],
            )
        )
        return moves

    def give_back(source, out, base, peers, own, at=slice(None)):
        moves = [
            remote(
                source.at[part(base + place(peer), cap), at],
                out.at[part(base + me_exp * cap, cap), at],
                exp=peer,
            )
            for peer in peers
        ]
        if own:
            moves.append(
                local(
                    source.at[part(base + place(me_exp), cap), at],
                    out.at[part(base + me_exp * cap, cap), at],
                )
            )
        begin(moves)
        return moves

    fill_table(0, ids_row[...])
    weight_col = jnp.sum(jnp.where(diagonal, weight_row[...], 0.0), axis=1, keepdims=True)
    loads[0].wait()
    scaled[...] = (weight_col * cot[...].astype(f32)).astype(bf)
    loads[1].wait()
    send_x[:rows] = dot(table[0], tok[0], NN).astype(bf)

    def gathered(own, out, at, at_peer, peer):
        return (
            remote(own.at[0], out.at[at], ctx=peer),
            remote(own.at[0], out.at[at], ctx=sib),
            remote(out.at[at_peer], out.at[at_peer], ctx=sib),
            local(own.at[0], out.at[at]),
        )

    at, at_across = cut(lax.rem(me, 4), cols), cut(lax.rem(across, 4), cols)
    side_w = [gathered(own, out, at, at_across, across) for own, out in ((w_gate, gate_w), (w_up, up_w))]
    side_w.append(gathered(w_down, down_w, side_y * 2 + core, (1 - side_y) * 2 + core, along))
    spread_x = [
        remote(ids_row, ids_far.at[0], ctx=along),
        remote(tok_in.at[:, other], tok.at[1], ctx=along),
    ]
    spread_y = [remote(ids_row, ids_far.at[1], ctx=across)] + [
        remote(
            scaled.at[:, cut(2 * s + 1 - side_x, strip)],
            scaled_far.at[:, s * strip:(s + 1) * strip],
            ctx=across,
        )
        for s in range(2)
    ]
    sent_x = [scatter(send_x, x_rows, base) for base in (0, rows)]
    sent_y = [scatter(send_y, y_rows, base) for base in (0, rows)]
    pl.semaphore_wait(pltpu.get_barrier_semaphore(), greeted)
    begin(spread_x)
    begin(spread_y)
    begin(sent_x[0])
    for g in side_w:
        g[0].start()
    for s in range(2):
        send_y[:rows, s * strip:(s + 1) * strip] = dot(
            table[0], scaled[:, cut(2 * s + side_x, strip)], NN
        ).astype(bf)
    spread_x[0].wait_recv()
    fill_table(1, ids_far[0])
    spread_x[1].wait_recv()
    send_x[rows:] = dot(table[1], tok[1], NN).astype(bf)
    begin(sent_x[1])
    for g in side_w:
        begin(g[1::2])
    spread_y[0].wait_recv()
    fill_table(2, ids_far[1])
    arrived(spread_y[1:])
    send_y[rows:] = dot(table[2], scaled_far[...], NN).astype(bf)

    def all_here(g):
        g[3].wait()
        g[1].wait_recv()
        g[2].wait_recv()

    def pass_on(g):
        g[0].wait_recv()
        g[2].start()

    pre_moves = [remote(pre_send.at[m], pre_got.at[m], ctx=along) for m in (0, 1)]
    pass_on(side_w[0])
    begin(sent_y[1])
    begin(sent_y[0])
    pass_on(side_w[2])
    arrived(sent_x[0])
    all_here(side_w[0])
    pre[0] = dot(x_rows[:rows], gate_w[...], NN)
    arrived(sent_x[1])
    pre_send[0] = dot(x_rows[rows:], gate_w[...], NN).astype(bf)
    pre_moves[0].start()
    pair = cut(core, 2 * rows)

    def pair_up(source, out):
        moves = []
        for q in range(2):
            moves.append(
                remote(source.at[:, cut(2 * q + 1 - core, cols)], out.at[q, pair], ctx=sib)
            )
            moves.append(local(source.at[:, cut(2 * q + core, cols)], out.at[q, pair]))
        begin(moves)
        return moves

    paired_x = pair_up(x_rows, x_two)
    all_here(side_w[2])
    for q in range(4):
        down_t[q * cols:(q + 1) * cols] = down_w[q].T
    pass_on(side_w[1])
    all_here(side_w[1])
    pre_send[1] = dot(x_rows[rows:], up_w[...], NN).astype(bf)
    pre_moves[1].start()
    pre[1] = dot(x_rows[:rows], up_w[...], NN)
    back_move = remote(back_send, back_got, ctx=across)
    arrived(sent_y[1])
    back_send[...] = dot(y_rows[rows:], down_t[...], NN).astype(bf)
    back_move.start()
    gate_t[...] = gate_w[...].T
    up_t[...] = up_w[...].T

    ours = part(core * 2 * rows, rows)
    theirs = part(core * 2 * rows + rows, rows)
    hid_across = remote(hid_all.at[ours], hid_all.at[theirs], ctx=across)
    hid_sib = [remote(hid_all.at[at], hid_all.at[at], ctx=sib) for at in (ours, theirs)]
    pre_moves[0].wait_recv()
    gate = pre[0] + pre_got[0].astype(f32)
    sig = 1.0 / (1.0 + jnp.exp(-gate))
    pre[0] = gate * sig
    slope[...] = sig * (1.0 + gate * (1.0 - sig))
    arrived(sent_y[0])
    paired_y = pair_up(y_rows, y_two)
    back_sum = dot(y_rows[:rows], down_t[...], NN)
    back_move.wait_recv()
    back_sum = back_sum + back_got[...].astype(f32)
    low = lax.rem(me_exp, 2)
    base = core * 2 * rows + rows
    halves = [part(base - rows + at * 2 * cap, 2 * cap) for at in (low, 1 - low)]
    far_halves = [part(base + at * 2 * cap, 2 * cap) for at in (low, 1 - low)]
    units = d_all.shape[2]
    pieces = [(1, pl.ds(0, units // 2)), (1, pl.ds(units // 2, units // 2)), (0, pl.ds(0, units))]
    first_along = [
        remote(d_all.at[1, ours, at], d_all.at[1, theirs, at], ctx=along) for _, at in pieces[:2]
    ]
    second_along = [
        remote(d_all.at[0, a], d_all.at[0, b], ctx=along) for a, b in zip(halves, far_halves)
    ]
    ours_sib = [remote(d_all.at[m, ours], d_all.at[m, ours], ctx=sib) for m in (0, 1)]
    theirs_sib = [
        remote(d_all.at[m, theirs, at], d_all.at[m, theirs, at], ctx=sib) for m, at in pieces
    ]
    d_all[1, ours] = (back_sum * pre[0]).astype(bf)
    begin(first_along)
    ours_sib[1].start()
    pre_moves[1].wait_recv()
    up = pre[1] + pre_got[1].astype(f32)
    d_all[0, ours] = (back_sum * up * slope[...]).astype(bf)
    begin(second_along)
    ours_sib[0].start()
    hid_all[ours] = (pre[0] * up).astype(bf)
    hid_across.start()
    hid_sib[0].start()

    def slot_rows(to, at):
        back[to] = (
            dot(d_all[0, at], gate_t[...], NN) + dot(d_all[1, at], up_t[...], NN)
        ).astype(bf)

    inner[...] = jnp.broadcast_to(
        jnp.sum(hid_all[ours].astype(f32) * back_sum, axis=1, keepdims=True), inner.shape
    )
    slot_rows(part(0, rows), ours)
    home_own = give_back(back, home, 0, exp_peers, True)
    home_own += give_back(inner, home_inner, 0, exp_peers, True)

    hid_across.wait_recv()
    hid_sib[1].start()
    arrived(paired_x)
    arrived(paired_y)
    sum_moves = [remote(sum_send.at[m, :, at], sum_got.at[m, :, at], ctx=across) for m, at in pieces]

    def side_sum(k):
        m, at = pieces[k]
        if k != 1:
            ours_sib[m].wait_recv()
        theirs_sib[k].wait_recv()
        sum_send[m, :, at] = dot(x_two[1 - side_x], d_all[m, :, at], TN).astype(bf)
        sum_moves[k].start()

    first_along[0].wait_recv()
    theirs_sib[0].start()
    side_sum(0)
    first_along[1].wait_recv()
    theirs_sib[1].start()
    arrived(hid_sib)
    down_move = remote(down_send, down_got, ctx=along)
    down_send[...] = dot(hid_all[...], y_two[1 - side_y], TN).astype(bf)
    down_move.start()
    side_sum(1)
    keep_down[...] = dot(hid_all[...], y_two[side_y], TN)
    keep[1] = dot(x_two[side_x], d_all[1], TN)
    second_along[0].wait_recv()
    slot_rows(part(rows + low * 2 * cap, 2 * cap), far_halves[0])
    home_far = give_back(back, home, rows, exp_peers[1:2], True)
    second_along[1].wait_recv()
    theirs_sib[2].start()
    slot_rows(part(rows + (1 - low) * 2 * cap, 2 * cap), far_halves[1])
    strips = [pl.ds(0, strip), pl.ds(strip, strip)]
    home_last = [give_back(back, home, rows, exp_peers[::2], False, at) for at in strips]
    side_sum(2)
    keep[0] = dot(x_two[side_x], d_all[0], TN)

    arrived(home_own)
    token_out[:, block] = dot(table[0], home[:rows], TN).astype(bf)
    route_out[...] = (
        jnp.sum(table[0].astype(f32) * home_inner[...], axis=0, keepdims=True) / weight_row[...]
    )
    arrived(home_far)
    tok_moves = [remote(tok_send.at[:, at], tok_got.at[:, at], ctx=along) for at in strips]
    for last, at, move in zip(home_last, strips, tok_moves):
        arrived(last)
        tok_send[:, at] = dot(table[1], home[rows:, at], TN).astype(bf)
        move.start()
    down_move.wait_recv()
    down_grad[...] = (keep_down[...] + down_got[...].astype(f32)).astype(bf)
    for m, out in ((1, up_grad), (0, gate_grad)):
        arrived(sum_moves[:2] if m else sum_moves[2:])
        out[...] = (keep[m] + sum_got[m].astype(f32)).astype(bf)
    arrived(tok_moves)
    token_out[:, other] = tok_got[...]
    copies.sent()


def hand_over(*refs):
    for source, out in zip(refs[:5], refs[5:]):
        out[...] = source[...]


def fast_body(tokens, cotangent, expert_ids, route_weights, w_gate, w_up, w_down):
    n_ctx = lax.axis_size("ctx")
    n_exp = lax.axis_size("exp")
    count, width = tokens.shape
    cap = max(2, (3 * count + 2 * n_exp - 1) // (2 * n_exp))
    cols = width // n_ctx
    units = w_gate.shape[2]
    rows = n_exp * cap
    wide = width // 2
    bf, f32 = jnp.bfloat16, jnp.float32
    vm = pl.BlockSpec(memory_space=pltpu.VMEM)
    hbm = pl.BlockSpec(memory_space=pl.ANY)
    dma = pltpu.SemaphoreType.DMA
    scratch = [
        ((2, count, wide), bf), ((count, width), bf), ((count, width), bf), ((count, wide), bf),
        ((2, 1, count), jnp.int32), ((3, rows, count), bf),
        ((2 * rows, wide), bf), ((2 * rows, wide), bf), ((2 * rows, wide), bf), ((2 * rows, wide), bf),
        ((wide, units), bf), ((wide, units), bf), ((n_ctx // 2, units, cols), bf),
        ((units, wide), bf), ((units, wide), bf), ((wide, units), bf),
        ((2, rows, units), bf), ((2, rows, units), bf), ((2, rows, units), f32),
        ((rows, units), f32),
        ((rows, units), bf), ((rows, units), bf),
        ((4 * rows, units), bf), ((2, 4 * rows, units), bf),
        ((2, 4 * rows, cols), bf), ((2, 4 * rows, cols), bf),
        ((2 * rows, wide), bf), ((2 * rows, wide), bf),
        ((rows, count), f32), ((rows, count), f32),
        ((2, cols, units), f32), ((2, cols, units), bf), ((2, cols, units), bf),
        ((units, cols), f32), ((units, cols), bf), ((units, cols), bf),
        ((count, wide), bf), ((count, wide), bf),
    ]
    token_grads, route, gate_grads, up_grads, down_grads = pl.pallas_call(
        functools.partial(kernel, n_exp, n_ctx, cap),
        out_shape=(
            jax.ShapeDtypeStruct((count, width), bf),
            jax.ShapeDtypeStruct((1, count), f32),
            jax.ShapeDtypeStruct((cols, units), bf),
            jax.ShapeDtypeStruct((cols, units), bf),
            jax.ShapeDtypeStruct((units, cols), bf),
        ),
        in_specs=[hbm] * 2 + [vm] * 2 + [hbm] * 3,
        out_specs=(vm,) * 5,
        scratch_shapes=[pltpu.VMEM(*one) for one in scratch] + [dma((80,)), dma((80,)), dma((40,))],
        compiler_params=pltpu.CompilerParams(
            collective_id=0, has_side_effects=True, vmem_limit_bytes=56 * 1024 * 1024
        ),
    )(
        tokens, cotangent, expert_ids.reshape(1, count), route_weights.reshape(1, count),
        w_gate, w_up, w_down,
    )
    results = (token_grads, route, gate_grads, up_grads, down_grads)
    token_grads, route, gate_grads, up_grads, down_grads = pl.pallas_call(
        hand_over,
        out_shape=tuple(jax.ShapeDtypeStruct(r.shape, r.dtype) for r in results),
        in_specs=[vm] * 5,
        out_specs=(vm,) * 5,
    )(*results)
    return (
        token_grads, route.reshape(count, 1), gate_grads[None], up_grads[None], down_grads[None]
    )


def solution(mesh):
    return jax.shard_map(
        fast_body if (mesh.shape["ctx"], mesh.shape["exp"]) == (8, 4) else body,
        mesh=mesh,
        in_specs=(
            P(("ctx", "exp"), None),
            P(("ctx", "exp"), None),
            P(("ctx", "exp"), None),
            P(("ctx", "exp"), None),
            P("exp", "ctx", None),
            P("exp", "ctx", None),
            P("exp", None, "ctx"),
        ),
        out_specs=(
            P(("ctx", "exp"), None),
            P(("ctx", "exp"), None),
            P("exp", "ctx", None),
            P("exp", "ctx", None),
            P("exp", None, "ctx"),
        ),
        check_vma=False,
    )
```

```python
import functools

import jax
import jax.numpy as jnp
from jax import lax
from jax.experimental import pallas as pl
from jax.experimental.pallas import tpu as pltpu
from jax.sharding import PartitionSpec as P

MESH = pl.DeviceIdType.MESH


def slot_table(route_ids, expert_count, capacity):
    labels = jnp.arange(expert_count, dtype=jnp.int32)
    onehot = (route_ids[..., :, None] == labels).astype(jnp.int32)
    position = jnp.sum((jnp.cumsum(onehot, axis=-2) - 1) * onehot, axis=-1)
    target = route_ids * capacity + position
    places = jnp.arange(expert_count * capacity, dtype=jnp.int32)
    return (target[..., None, :] == places[:, None]).astype(jnp.bfloat16)


def forward_hidden(totals, units):
    gate_pre = totals[:, :units]
    up_pre = totals[:, units:]
    gate_sig = jax.nn.sigmoid(gate_pre)
    return (gate_pre * gate_sig * up_pre).astype(jnp.bfloat16)


def backward_grads(totals, back_sum, units):
    gate_pre = totals[:, :units]
    up_pre = totals[:, units:]
    gate_sig = jax.nn.sigmoid(gate_pre)
    d_up = (back_sum * gate_pre * gate_sig).astype(jnp.bfloat16)
    d_gate = (back_sum * up_pre * gate_sig * (1.0 + gate_pre * (1.0 - gate_sig))).astype(
        jnp.bfloat16
    )
    return jnp.concatenate([d_gate, d_up], axis=1)


def body(tokens, cotangent, expert_ids, route_weights, w_gate, w_up, w_down):
    ctx_size = lax.axis_size("ctx")
    exp_size = lax.axis_size("exp")
    tok_count, model_width = tokens.shape
    route_count = expert_ids.shape[1]
    slot_count = tok_count * route_count
    expert_count = w_gate.shape[0] * exp_size
    capacity = max(2, (3 * slot_count + 2 * expert_count - 1) // (2 * expert_count))
    col_count = model_width // ctx_size
    units = w_gate.shape[2]
    row_count = ctx_size * exp_size * capacity
    own_rows = row_count // ctx_size
    all_ids = lax.all_gather(expert_ids, "ctx", axis=0, tiled=True)
    tables = slot_table(all_ids.reshape(ctx_size, slot_count), expert_count, capacity)
    token_slots = jnp.repeat(tokens, route_count, axis=0)
    scaled = (
        route_weights * jnp.repeat(cotangent, route_count, axis=0).astype(jnp.float32)
    ).astype(jnp.bfloat16)
    own_table = lax.dynamic_index_in_dim(tables, lax.axis_index("ctx"), 0, keepdims=False)
    send_x = jnp.dot(own_table, token_slots, preferred_element_type=jnp.float32).astype(
        jnp.bfloat16
    )
    send_y = jnp.dot(own_table, scaled, preferred_element_type=jnp.float32).astype(jnp.bfloat16)
    send_x = send_x.reshape(expert_count, capacity, model_width)
    send_y = send_y.reshape(expert_count, capacity, model_width)
    group_x, group_y = (
        lax.all_to_all(send_x, "exp", split_axis=0, concat_axis=0, tiled=True),
        lax.all_to_all(send_y, "exp", split_axis=0, concat_axis=0, tiled=True),
    )
    slot_x, slot_y = (
        lax.all_to_all(group_x, "ctx", split_axis=2, concat_axis=0, tiled=True),
        lax.all_to_all(group_y, "ctx", split_axis=2, concat_axis=0, tiled=True),
    )
    slot_x = slot_x.reshape(row_count, col_count)
    slot_y = slot_y.reshape(row_count, col_count)
    gate_weight = w_gate[0]
    up_weight = w_up[0]
    down_weight = w_down[0]
    both_weights = jnp.concatenate([gate_weight, up_weight], axis=1)

    def fold_grad(segment):
        gate_acc = lax.dot_general(
            slot_x, segment[:, :units], (((0,), (0,)), ((), ())), preferred_element_type=jnp.float32
        )
        up_acc = lax.dot_general(
            slot_x, segment[:, units:], (((0,), (0,)), ((), ())), preferred_element_type=jnp.float32
        )
        grad_rows = lax.dot_general(
            segment, both_weights, (((1,), (1,)), ((), ())), preferred_element_type=jnp.float32
        )
        return (gate_acc, up_acc, grad_rows)

    row_x, row_y = (
        lax.all_to_all(slot_x, "ctx", split_axis=0, concat_axis=1, tiled=True),
        lax.all_to_all(slot_y, "ctx", split_axis=0, concat_axis=1, tiled=True),
    )
    full_gate, full_up, full_down = (
        lax.all_gather(gate_weight, "ctx", axis=0, tiled=True),
        lax.all_gather(up_weight, "ctx", axis=0, tiled=True),
        lax.all_gather(down_weight, "ctx", axis=1, tiled=True),
    )
    full_both = jnp.concatenate([full_gate, full_up], axis=1).reshape(
        ctx_size, col_count, 2 * units
    )
    gate_blocks = jnp.einsum(
        "rcd,cdf->crf",
        row_x.reshape(own_rows, ctx_size, col_count),
        full_both,
        preferred_element_type=jnp.float32,
    ).astype(jnp.bfloat16)
    totals_own = jnp.sum(gate_blocks.astype(jnp.float32), axis=0)
    hidden_own = forward_hidden(totals_own, units)
    back_blocks = jnp.einsum(
        "rcd,fcd->crf",
        row_y.reshape(own_rows, ctx_size, col_count),
        full_down.reshape(units, ctx_size, col_count),
        preferred_element_type=jnp.float32,
    ).astype(jnp.bfloat16)
    back_own = jnp.sum(back_blocks.astype(jnp.float32), axis=0)
    grads_own = backward_grads(totals_own, back_own, units)
    segment = (
        lax.all_gather(hidden_own, "ctx", axis=0, tiled=True),
        lax.all_gather(grads_own, "ctx", axis=0, tiled=True),
    )
    fold_segment = segment[0]
    outputs = jnp.dot(fold_segment, down_weight, preferred_element_type=jnp.float32)
    inner_rows = jnp.sum(slot_y.astype(jnp.float32) * outputs, axis=1)
    inner_all = inner_rows
    down_acc = lax.dot_general(
        fold_segment, slot_y, (((0,), (0,)), ((), ())), preferred_element_type=jnp.float32
    )
    down_state = (down_acc, inner_all)
    grad_state = fold_grad(segment[1])
    down_acc = down_state[0]
    inner_all = down_state[1]
    gate_acc = grad_state[0]
    up_acc = grad_state[1]
    back_rows = grad_state[2]
    back_slots = back_rows.astype(jnp.bfloat16).reshape(ctx_size, exp_size, capacity, col_count)
    inner_slots = inner_all.reshape(ctx_size, exp_size, capacity)
    home_back = lax.all_to_all(back_slots, "exp", split_axis=1, concat_axis=1, tiled=True)
    home_inner = lax.all_to_all(inner_slots, "exp", split_axis=1, concat_axis=1, tiled=True)
    merged = jnp.einsum(
        "cks,ckd->csd",
        tables,
        home_back.reshape(ctx_size, expert_count * capacity, col_count),
        preferred_element_type=jnp.float32,
    )
    merged = jnp.sum(merged.reshape(ctx_size, tok_count, route_count, col_count), axis=2).astype(
        jnp.bfloat16
    )
    grads_home = lax.all_to_all(merged, "ctx", split_axis=0, concat_axis=2, tiled=True)
    token_grads = grads_home.reshape(tok_count, model_width)
    inner_home = jnp.einsum(
        "cks,ck->cs",
        tables.astype(jnp.float32),
        home_inner.reshape(ctx_size, expert_count * capacity),
        precision=lax.Precision.HIGHEST,
    )
    route_sums = lax.psum_scatter(inner_home, "ctx", scatter_dimension=0, tiled=True).reshape(
        tok_count, route_count
    )
    route_grads = route_sums / route_weights
    gate_grads = gate_acc.astype(jnp.bfloat16)[None]
    up_grads = up_acc.astype(jnp.bfloat16)[None]
    down_grads = down_acc.astype(jnp.bfloat16)[None]
    return (token_grads, route_grads, gate_grads, up_grads, down_grads)


def ctx_neighbours(me):
    sib = me + 1 - 2 * (me % 2)
    across = me + 2 - 4 * ((me // 2) % 2)
    along = me + 4 - 8 * ((me // 4) % 2)
    return sib, across, along


def greet(ctx_peers, exp_peers):
    barrier = pltpu.get_barrier_semaphore()
    for peer in ctx_peers:
        pl.semaphore_signal(barrier, inc=1, device_id={"ctx": peer}, device_id_type=MESH)
    for peer in exp_peers:
        pl.semaphore_signal(barrier, inc=1, device_id={"exp": peer}, device_id_type=MESH)
    return len(ctx_peers) + len(exp_peers)


class Copies:
    def __init__(self, send_sem, recv_sem, local_sem):
        self.sems = send_sem, recv_sem, local_sem
        self.far, self.near = [], 0

    def remote(self, source, target, **peer):
        k = len(self.far)
        one = pltpu.make_async_remote_copy(
            src_ref=source,
            dst_ref=target,
            send_sem=self.sems[0].at[k],
            recv_sem=self.sems[1].at[k],
            device_id=peer,
            device_id_type=MESH,
        )
        self.far.append(one)
        return one

    def local(self, source, target):
        one = pltpu.make_async_copy(source, target, self.sems[2].at[self.near])
        self.near += 1
        return one

    def sent(self):
        for one in self.far:
            one.wait_send()


def begin(copies):
    for one in copies:
        one.start()


def arrived(copies):
    for one in copies:
        one.wait_recv()


NT = (((1,), (1,)), ((), ()))
TN = (((0,), (0,)), ((), ()))
NN = (((1,), (0,)), ((), ()))


def dot(a, b, dims):
    return lax.dot_general(a, b, dims, preferred_element_type=jnp.float32)


def kernel(
    n_exp, n_ctx, cap,
    tok_in, cot_in, ids_row, weight_row, w_gate, w_up, w_down,
    token_out, route_out, gate_grad, up_grad, down_grad,
    tok, cot, scaled, scaled_far, ids_far, table, send_x, x_rows, send_y, y_rows,
    gate_w, up_w, down_w, gate_t, up_t, down_t,
    pre_send, pre_got, pre, slope, back_send, back_got, hid_all, d_all, x_two, y_two,
    back, home, inner, home_inner,
    keep, sum_send, sum_got, keep_down, down_send, down_got, tok_send, tok_got,
    send_sem, recv_sem, local_sem,
):
    me_exp = lax.axis_index("exp")
    me = lax.axis_index("ctx")
    bf, f32 = jnp.bfloat16, jnp.float32
    sib, across, along = ctx_neighbours(me)
    core = lax.rem(me, 2)
    side_x = lax.rem(lax.div(me, 2), 2)
    side_y = lax.div(me, 4)
    exp_peers = [lax.rem(me_exp + d, n_exp) for d in range(1, n_exp)]
    count, width = cot.shape
    cols = width // n_ctx
    rows = n_exp * cap
    wide, strip = width // 2, width // 4

    def cut(at, size):
        return pl.ds(pl.multiple_of(at * size, size), size)

    def part(base, size):
        return pl.ds(pl.multiple_of(base, 16), size)

    copies = Copies(send_sem, recv_sem, local_sem)
    remote, local = copies.remote, copies.local
    block, other = cut(side_y, wide), cut(1 - side_y, wide)
    loads = [local(cot_in, cot), local(tok_in.at[:, block], tok.at[0])]
    begin(loads)
    greeted = greet([sib, across, along], exp_peers)

    down_i = lax.broadcasted_iota(jnp.int32, (count, count), 0)
    over_i = lax.broadcasted_iota(jnp.int32, (count, count), 1)
    diagonal = down_i == over_i

    def fill_table(at, row):
        row_f = row.astype(f32)
        col_f = jnp.sum(jnp.where(diagonal, row_f, 0.0), axis=1, keepdims=True)
        position = jnp.sum(
            jnp.where((col_f == row_f) & (down_i < over_i), 1.0, 0.0), axis=0, keepdims=True
        )
        target = row * cap + position.astype(jnp.int32)
        places = lax.broadcasted_iota(jnp.int32, (rows, count), 0)
        table[at] = jnp.where(places == target, 1.0, 0.0).astype(bf)

    def place(at):
        return (lax.rem(at, 2) * 2 + lax.div(at, 2)) * cap

    def scatter(source, out, base):
        moves = [
            remote(
                source.at[part(base + peer * cap, cap)],
                out.at[part(base + place(me_exp), cap)],
                exp=peer,
            )
            for peer in exp_peers
        ]
        moves.append(
            local(
                source.at[part(base + me_exp * cap, cap)],
                out.at[part(base + place(me_exp), cap)],
            )
        )
        return moves

    def give_back(source, out, base, peers, own, at=slice(None)):
        moves = [
            remote(
                source.at[part(base + place(peer), cap), at],
                out.at[part(base + me_exp * cap, cap), at],
                exp=peer,
            )
            for peer in peers
        ]
        if own:
            moves.append(
                local(
                    source.at[part(base + place(me_exp), cap), at],
                    out.at[part(base + me_exp * cap, cap), at],
                )
            )
        begin(moves)
        return moves

    fill_table(0, ids_row[...])
    weight_col = jnp.sum(jnp.where(diagonal, weight_row[...], 0.0), axis=1, keepdims=True)
    loads[0].wait()
    scaled[...] = (weight_col * cot[...].astype(f32)).astype(bf)
    loads[1].wait()
    send_x[:rows] = dot(table[0], tok[0], NN).astype(bf)

    def gathered(own, out, at, at_peer, peer):
        return (
            remote(own.at[0], out.at[at], ctx=peer),
            remote(own.at[0], out.at[at], ctx=sib),
            remote(out.at[at_peer], out.at[at_peer], ctx=sib),
            local(own.at[0], out.at[at]),
        )

    at, at_across = cut(lax.rem(me, 4), cols), cut(lax.rem(across, 4), cols)
    side_w = [gathered(own, out, at, at_across, across) for own, out in ((w_gate, gate_w), (w_up, up_w))]
    side_w.append(gathered(w_down, down_w, side_y * 2 + core, (1 - side_y) * 2 + core, along))
    spread_x = [
        remote(ids_row, ids_far.at[0], ctx=along),
        remote(tok_in.at[:, other], tok.at[1], ctx=along),
    ]
    spread_y = [remote(ids_row, ids_far.at[1], ctx=across)] + [
        remote(
            scaled.at[:, cut(2 * s + 1 - side_x, strip)],
            scaled_far.at[:, s * strip:(s + 1) * strip],
            ctx=across,
        )
        for s in range(2)
    ]
    sent_x = [scatter(send_x, x_rows, base) for base in (0, rows)]
    sent_y = [scatter(send_y, y_rows, base) for base in (0, rows)]
    pl.semaphore_wait(pltpu.get_barrier_semaphore(), greeted)
    begin(spread_x)
    begin(spread_y)
    begin(sent_x[0])
    for g in side_w:
        g[0].start()
    for s in range(2):
        send_y[:rows, s * strip:(s + 1) * strip] = dot(
            table[0], scaled[:, cut(2 * s + side_x, strip)], NN
        ).astype(bf)
    spread_x[0].wait_recv()
    fill_table(1, ids_far[0])
    spread_x[1].wait_recv()
    send_x[rows:] = dot(table[1], tok[1], NN).astype(bf)
    begin(sent_x[1])
    for g in side_w:
        begin(g[1::2])
    spread_y[0].wait_recv()
    fill_table(2, ids_far[1])
    arrived(spread_y[1:])
    send_y[rows:] = dot(table[2], scaled_far[...], NN).astype(bf)

    def all_here(g):
        g[3].wait()
        g[1].wait_recv()
        g[2].wait_recv()

    def pass_on(g):
        g[0].wait_recv()
        g[2].start()

    pre_moves = [remote(pre_send.at[m], pre_got.at[m], ctx=along) for m in (0, 1)]
    pass_on(side_w[0])
    begin(sent_y[1])
    pass_on(side_w[2])
    arrived(sent_x[0])
    all_here(side_w[0])
    pre[0] = dot(x_rows[:rows], gate_w[...], NN)
    begin(sent_y[0])
    arrived(sent_x[1])
    pre_send[0] = dot(x_rows[rows:], gate_w[...], NN).astype(bf)
    pre_moves[0].start()
    pair = cut(core, 2 * rows)

    def pair_up(source, out):
        moves = []
        for q in range(2):
            moves.append(
                remote(source.at[:, cut(2 * q + 1 - core, cols)], out.at[q, pair], ctx=sib)
            )
            moves.append(local(source.at[:, cut(2 * q + core, cols)], out.at[q, pair]))
        begin(moves)
        return moves

    paired_x = pair_up(x_rows, x_two)
    all_here(side_w[2])
    for q in range(4):
        down_t[q * cols:(q + 1) * cols] = down_w[q].T
    pass_on(side_w[1])
    all_here(side_w[1])
    pre_send[1] = dot(x_rows[rows:], up_w[...], NN).astype(bf)
    pre_moves[1].start()
    pre[1] = dot(x_rows[:rows], up_w[...], NN)
    back_move = remote(back_send, back_got, ctx=across)
    arrived(sent_y[1])
    back_send[...] = dot(y_rows[rows:], down_t[...], NN).astype(bf)
    back_move.start()
    gate_t[...] = gate_w[...].T
    up_t[...] = up_w[...].T

    ours = part(core * 2 * rows, rows)
    theirs = part(core * 2 * rows + rows, rows)
    hid_across = remote(hid_all.at[ours], hid_all.at[theirs], ctx=across)
    hid_sib = [remote(hid_all.at[at], hid_all.at[at], ctx=sib) for at in (ours, theirs)]
    pre_moves[0].wait_recv()
    gate = pre[0] + pre_got[0].astype(f32)
    sig = 1.0 / (1.0 + jnp.exp(-gate))
    pre[0] = gate * sig
    slope[...] = sig * (1.0 + gate * (1.0 - sig))
    arrived(sent_y[0])
    paired_y = pair_up(y_rows, y_two)
    back_sum = dot(y_rows[:rows], down_t[...], NN)
    back_move.wait_recv()
    back_sum = back_sum + back_got[...].astype(f32)
    low = lax.rem(me_exp, 2)
    base = core * 2 * rows + rows
    halves = [part(base - rows + at * 2 * cap, 2 * cap) for at in (low, 1 - low)]
    far_halves = [part(base + at * 2 * cap, 2 * cap) for at in (low, 1 - low)]
    units = d_all.shape[2]
    pieces = [(1, pl.ds(0, units // 2)), (1, pl.ds(units // 2, units // 2)), (0, pl.ds(0, units))]
    first_along = [
        remote(d_all.at[1, ours, at], d_all.at[1, theirs, at], ctx=along) for _, at in pieces[:2]
    ]
    second_along = [
        remote(d_all.at[0, a], d_all.at[0, b], ctx=along) for a, b in zip(halves, far_halves)
    ]
    ours_sib = [remote(d_all.at[m, ours], d_all.at[m, ours], ctx=sib) for m in (0, 1)]
    theirs_sib = [
        remote(d_all.at[m, theirs, at], d_all.at[m, theirs, at], ctx=sib) for m, at in pieces
    ]
    d_all[1, ours] = (back_sum * pre[0]).astype(bf)
    begin(first_along)
    ours_sib[1].start()
    pre_moves[1].wait_recv()
    up = pre[1] + pre_got[1].astype(f32)
    d_all[0, ours] = (back_sum * up * slope[...]).astype(bf)
    begin(second_along)
    ours_sib[0].start()
    hid_all[ours] = (pre[0] * up).astype(bf)
    hid_across.start()
    hid_sib[0].start()

    def slot_rows(to, at):
        back[to] = (
            dot(d_all[0, at], gate_t[...], NN) + dot(d_all[1, at], up_t[...], NN)
        ).astype(bf)

    inner[...] = jnp.broadcast_to(
        jnp.sum(hid_all[ours].astype(f32) * back_sum, axis=1, keepdims=True), inner.shape
    )
    slot_rows(part(0, rows), ours)
    home_own = give_back(back, home, 0, exp_peers, True)
    home_own += give_back(inner, home_inner, 0, exp_peers, True)

    hid_across.wait_recv()
    hid_sib[1].start()
    arrived(paired_x)
    arrived(paired_y)
    sum_moves = [remote(sum_send.at[m, :, at], sum_got.at[m, :, at], ctx=across) for m, at in pieces]

    def side_sum(k):
        m, at = pieces[k]
        if k != 1:
            ours_sib[m].wait_recv()
        theirs_sib[k].wait_recv()
        sum_send[m, :, at] = dot(x_two[1 - side_x], d_all[m, :, at], TN).astype(bf)
        sum_moves[k].start()

    first_along[0].wait_recv()
    theirs_sib[0].start()
    side_sum(0)
    first_along[1].wait_recv()
    theirs_sib[1].start()
    arrived(hid_sib)
    down_move = remote(down_send, down_got, ctx=along)
    down_send[...] = dot(hid_all[...], y_two[1 - side_y], TN).astype(bf)
    down_move.start()
    side_sum(1)
    keep_down[...] = dot(hid_all[...], y_two[side_y], TN)
    keep[1] = dot(x_two[side_x], d_all[1], TN)
    second_along[0].wait_recv()
    slot_rows(part(rows + low * 2 * cap, 2 * cap), far_halves[0])
    home_far = give_back(back, home, rows, exp_peers[1:2], True)
    second_along[1].wait_recv()
    theirs_sib[2].start()
    slot_rows(part(rows + (1 - low) * 2 * cap, 2 * cap), far_halves[1])
    strips = [pl.ds(q * cols, cols) for q in range(4)]
    home_last = [give_back(back, home, rows, exp_peers[::2], False, at) for at in strips]
    side_sum(2)
    keep[0] = dot(x_two[side_x], d_all[0], TN)

    arrived(home_own)
    token_out[:, block] = dot(table[0], home[:rows], TN).astype(bf)
    route_out[...] = (
        jnp.sum(table[0].astype(f32) * home_inner[...], axis=0, keepdims=True) / weight_row[...]
    )
    arrived(home_far)
    tok_moves = [remote(tok_send.at[:, at], tok_got.at[:, at], ctx=along) for at in strips]
    for last, at, move in zip(home_last, strips, tok_moves):
        arrived(last)
        tok_send[:, at] = dot(table[1], home[rows:, at], TN).astype(bf)
        move.start()
    down_move.wait_recv()
    down_grad[...] = (keep_down[...] + down_got[...].astype(f32)).astype(bf)
    for m, out in ((1, up_grad), (0, gate_grad)):
        arrived(sum_moves[:2] if m else sum_moves[2:])
        out[...] = (keep[m] + sum_got[m].astype(f32)).astype(bf)
    arrived(tok_moves)
    token_out[:, other] = tok_got[...]
    copies.sent()


def hand_over(*refs):
    for source, out in zip(refs[:5], refs[5:]):
        out[...] = source[...]


def fast_body(tokens, cotangent, expert_ids, route_weights, w_gate, w_up, w_down):
    n_ctx = lax.axis_size("ctx")
    n_exp = lax.axis_size("exp")
    count, width = tokens.shape
    cap = max(2, (3 * count + 2 * n_exp - 1) // (2 * n_exp))
    cols = width // n_ctx
    units = w_gate.shape[2]
    rows = n_exp * cap
    wide = width // 2
    bf, f32 = jnp.bfloat16, jnp.float32
    vm = pl.BlockSpec(memory_space=pltpu.VMEM)
    hbm = pl.BlockSpec(memory_space=pl.ANY)
    dma = pltpu.SemaphoreType.DMA
    scratch = [
        ((2, count, wide), bf), ((count, width), bf), ((count, width), bf), ((count, wide), bf),
        ((2, 1, count), jnp.int32), ((3, rows, count), bf),
        ((2 * rows, wide), bf), ((2 * rows, wide), bf), ((2 * rows, wide), bf), ((2 * rows, wide), bf),
        ((wide, units), bf), ((wide, units), bf), ((n_ctx // 2, units, cols), bf),
        ((units, wide), bf), ((units, wide), bf), ((wide, units), bf),
        ((2, rows, units), bf), ((2, rows, units), bf), ((2, rows, units), f32),
        ((rows, units), f32),
        ((rows, units), bf), ((rows, units), bf),
        ((4 * rows, units), bf), ((2, 4 * rows, units), bf),
        ((2, 4 * rows, cols), bf), ((2, 4 * rows, cols), bf),
        ((2 * rows, wide), bf), ((2 * rows, wide), bf),
        ((rows, count), f32), ((rows, count), f32),
        ((2, cols, units), f32), ((2, cols, units), bf), ((2, cols, units), bf),
        ((units, cols), f32), ((units, cols), bf), ((units, cols), bf),
        ((count, wide), bf), ((count, wide), bf),
    ]
    token_grads, route, gate_grads, up_grads, down_grads = pl.pallas_call(
        functools.partial(kernel, n_exp, n_ctx, cap),
        out_shape=(
            jax.ShapeDtypeStruct((count, width), bf),
            jax.ShapeDtypeStruct((1, count), f32),
            jax.ShapeDtypeStruct((cols, units), bf),
            jax.ShapeDtypeStruct((cols, units), bf),
            jax.ShapeDtypeStruct((units, cols), bf),
        ),
        in_specs=[hbm] * 2 + [vm] * 2 + [hbm] * 3,
        out_specs=(vm,) * 5,
        scratch_shapes=[pltpu.VMEM(*one) for one in scratch] + [dma((80,)), dma((80,)), dma((40,))],
        compiler_params=pltpu.CompilerParams(
            collective_id=0, has_side_effects=True, vmem_limit_bytes=56 * 1024 * 1024
        ),
    )(
        tokens, cotangent, expert_ids.reshape(1, count), route_weights.reshape(1, count),
        w_gate, w_up, w_down,
    )
    results = (token_grads, route, gate_grads, up_grads, down_grads)
    token_grads, route, gate_grads, up_grads, down_grads = pl.pallas_call(
        hand_over,
        out_shape=tuple(jax.ShapeDtypeStruct(r.shape, r.dtype) for r in results),
        in_specs=[vm] * 5,
        out_specs=(vm,) * 5,
    )(*results)
    return (
        token_grads, route.reshape(count, 1), gate_grads[None], up_grads[None], down_grads[None]
    )


def solution(mesh):
    return jax.shard_map(
        fast_body if (mesh.shape["ctx"], mesh.shape["exp"]) == (8, 4) else body,
        mesh=mesh,
        in_specs=(
            P(("ctx", "exp"), None),
            P(("ctx", "exp"), None),
            P(("ctx", "exp"), None),
            P(("ctx", "exp"), None),
            P("exp", "ctx", None),
            P("exp", "ctx", None),
            P("exp", None, "ctx"),
        ),
        out_specs=(
            P(("ctx", "exp"), None),
            P(("ctx", "exp"), None),
            P("exp", "ctx", None),
            P("exp", "ctx", None),
            P("exp", None, "ctx"),
        ),
        check_vma=False,
    )
```

```python
import functools

import jax
import jax.numpy as jnp
from jax import lax
from jax.experimental import pallas as pl
from jax.experimental.pallas import tpu as pltpu
from jax.sharding import PartitionSpec as P

MESH = pl.DeviceIdType.MESH


def slot_table(route_ids, expert_count, capacity):
    labels = jnp.arange(expert_count, dtype=jnp.int32)
    onehot = (route_ids[..., :, None] == labels).astype(jnp.int32)
    position = jnp.sum((jnp.cumsum(onehot, axis=-2) - 1) * onehot, axis=-1)
    target = route_ids * capacity + position
    places = jnp.arange(expert_count * capacity, dtype=jnp.int32)
    return (target[..., None, :] == places[:, None]).astype(jnp.bfloat16)


def forward_hidden(totals, units):
    gate_pre = totals[:, :units]
    up_pre = totals[:, units:]
    gate_sig = jax.nn.sigmoid(gate_pre)
    return (gate_pre * gate_sig * up_pre).astype(jnp.bfloat16)


def backward_grads(totals, back_sum, units):
    gate_pre = totals[:, :units]
    up_pre = totals[:, units:]
    gate_sig = jax.nn.sigmoid(gate_pre)
    d_up = (back_sum * gate_pre * gate_sig).astype(jnp.bfloat16)
    d_gate = (back_sum * up_pre * gate_sig * (1.0 + gate_pre * (1.0 - gate_sig))).astype(
        jnp.bfloat16
    )
    return jnp.concatenate([d_gate, d_up], axis=1)


def body(tokens, cotangent, expert_ids, route_weights, w_gate, w_up, w_down):
    ctx_size = lax.axis_size("ctx")
    exp_size = lax.axis_size("exp")
    tok_count, model_width = tokens.shape
    route_count = expert_ids.shape[1]
    slot_count = tok_count * route_count
    expert_count = w_gate.shape[0] * exp_size
    capacity = max(2, (3 * slot_count + 2 * expert_count - 1) // (2 * expert_count))
    col_count = model_width // ctx_size
    units = w_gate.shape[2]
    row_count = ctx_size * exp_size * capacity
    own_rows = row_count // ctx_size
    all_ids = lax.all_gather(expert_ids, "ctx", axis=0, tiled=True)
    tables = slot_table(all_ids.reshape(ctx_size, slot_count), expert_count, capacity)
    token_slots = jnp.repeat(tokens, route_count, axis=0)
    scaled = (
        route_weights * jnp.repeat(cotangent, route_count, axis=0).astype(jnp.float32)
    ).astype(jnp.bfloat16)
    own_table = lax.dynamic_index_in_dim(tables, lax.axis_index("ctx"), 0, keepdims=False)
    send_x = jnp.dot(own_table, token_slots, preferred_element_type=jnp.float32).astype(
        jnp.bfloat16
    )
    send_y = jnp.dot(own_table, scaled, preferred_element_type=jnp.float32).astype(jnp.bfloat16)
    send_x = send_x.reshape(expert_count, capacity, model_width)
    send_y = send_y.reshape(expert_count, capacity, model_width)
    group_x, group_y = (
        lax.all_to_all(send_x, "exp", split_axis=0, concat_axis=0, tiled=True),
        lax.all_to_all(send_y, "exp", split_axis=0, concat_axis=0, tiled=True),
    )
    slot_x, slot_y = (
        lax.all_to_all(group_x, "ctx", split_axis=2, concat_axis=0, tiled=True),
        lax.all_to_all(group_y, "ctx", split_axis=2, concat_axis=0, tiled=True),
    )
    slot_x = slot_x.reshape(row_count, col_count)
    slot_y = slot_y.reshape(row_count, col_count)
    gate_weight = w_gate[0]
    up_weight = w_up[0]
    down_weight = w_down[0]
    both_weights = jnp.concatenate([gate_weight, up_weight], axis=1)

    def fold_grad(segment):
        gate_acc = lax.dot_general(
            slot_x, segment[:, :units], (((0,), (0,)), ((), ())), preferred_element_type=jnp.float32
        )
        up_acc = lax.dot_general(
            slot_x, segment[:, units:], (((0,), (0,)), ((), ())), preferred_element_type=jnp.float32
        )
        grad_rows = lax.dot_general(
            segment, both_weights, (((1,), (1,)), ((), ())), preferred_element_type=jnp.float32
        )
        return (gate_acc, up_acc, grad_rows)

    row_x, row_y = (
        lax.all_to_all(slot_x, "ctx", split_axis=0, concat_axis=1, tiled=True),
        lax.all_to_all(slot_y, "ctx", split_axis=0, concat_axis=1, tiled=True),
    )
    full_gate, full_up, full_down = (
        lax.all_gather(gate_weight, "ctx", axis=0, tiled=True),
        lax.all_gather(up_weight, "ctx", axis=0, tiled=True),
        lax.all_gather(down_weight, "ctx", axis=1, tiled=True),
    )
    full_both = jnp.concatenate([full_gate, full_up], axis=1).reshape(
        ctx_size, col_count, 2 * units
    )
    gate_blocks = jnp.einsum(
        "rcd,cdf->crf",
        row_x.reshape(own_rows, ctx_size, col_count),
        full_both,
        preferred_element_type=jnp.float32,
    ).astype(jnp.bfloat16)
    totals_own = jnp.sum(gate_blocks.astype(jnp.float32), axis=0)
    hidden_own = forward_hidden(totals_own, units)
    back_blocks = jnp.einsum(
        "rcd,fcd->crf",
        row_y.reshape(own_rows, ctx_size, col_count),
        full_down.reshape(units, ctx_size, col_count),
        preferred_element_type=jnp.float32,
    ).astype(jnp.bfloat16)
    back_own = jnp.sum(back_blocks.astype(jnp.float32), axis=0)
    grads_own = backward_grads(totals_own, back_own, units)
    segment = (
        lax.all_gather(hidden_own, "ctx", axis=0, tiled=True),
        lax.all_gather(grads_own, "ctx", axis=0, tiled=True),
    )
    fold_segment = segment[0]
    outputs = jnp.dot(fold_segment, down_weight, preferred_element_type=jnp.float32)
    inner_rows = jnp.sum(slot_y.astype(jnp.float32) * outputs, axis=1)
    inner_all = inner_rows
    down_acc = lax.dot_general(
        fold_segment, slot_y, (((0,), (0,)), ((), ())), preferred_element_type=jnp.float32
    )
    down_state = (down_acc, inner_all)
    grad_state = fold_grad(segment[1])
    down_acc = down_state[0]
    inner_all = down_state[1]
    gate_acc = grad_state[0]
    up_acc = grad_state[1]
    back_rows = grad_state[2]
    back_slots = back_rows.astype(jnp.bfloat16).reshape(ctx_size, exp_size, capacity, col_count)
    inner_slots = inner_all.reshape(ctx_size, exp_size, capacity)
    home_back = lax.all_to_all(back_slots, "exp", split_axis=1, concat_axis=1, tiled=True)
    home_inner = lax.all_to_all(inner_slots, "exp", split_axis=1, concat_axis=1, tiled=True)
    merged = jnp.einsum(
        "cks,ckd->csd",
        tables,
        home_back.reshape(ctx_size, expert_count * capacity, col_count),
        preferred_element_type=jnp.float32,
    )
    merged = jnp.sum(merged.reshape(ctx_size, tok_count, route_count, col_count), axis=2).astype(
        jnp.bfloat16
    )
    grads_home = lax.all_to_all(merged, "ctx", split_axis=0, concat_axis=2, tiled=True)
    token_grads = grads_home.reshape(tok_count, model_width)
    inner_home = jnp.einsum(
        "cks,ck->cs",
        tables.astype(jnp.float32),
        home_inner.reshape(ctx_size, expert_count * capacity),
        precision=lax.Precision.HIGHEST,
    )
    route_sums = lax.psum_scatter(inner_home, "ctx", scatter_dimension=0, tiled=True).reshape(
        tok_count, route_count
    )
    route_grads = route_sums / route_weights
    gate_grads = gate_acc.astype(jnp.bfloat16)[None]
    up_grads = up_acc.astype(jnp.bfloat16)[None]
    down_grads = down_acc.astype(jnp.bfloat16)[None]
    return (token_grads, route_grads, gate_grads, up_grads, down_grads)


def ctx_neighbours(me):
    sib = me + 1 - 2 * (me % 2)
    across = me + 2 - 4 * ((me // 2) % 2)
    along = me + 4 - 8 * ((me // 4) % 2)
    return sib, across, along


def greet(ctx_peers, exp_peers):
    barrier = pltpu.get_barrier_semaphore()
    for peer in ctx_peers:
        pl.semaphore_signal(barrier, inc=1, device_id={"ctx": peer}, device_id_type=MESH)
    for peer in exp_peers:
        pl.semaphore_signal(barrier, inc=1, device_id={"exp": peer}, device_id_type=MESH)
    return len(ctx_peers) + len(exp_peers)


class Copies:
    def __init__(self, send_sem, recv_sem, local_sem):
        self.sems = send_sem, recv_sem, local_sem
        self.far, self.near = [], 0

    def remote(self, source, target, **peer):
        k = len(self.far)
        one = pltpu.make_async_remote_copy(
            src_ref=source,
            dst_ref=target,
            send_sem=self.sems[0].at[k],
            recv_sem=self.sems[1].at[k],
            device_id=peer,
            device_id_type=MESH,
        )
        self.far.append(one)
        return one

    def local(self, source, target):
        one = pltpu.make_async_copy(source, target, self.sems[2].at[self.near])
        self.near += 1
        return one

    def sent(self):
        for one in self.far:
            one.wait_send()


def begin(copies):
    for one in copies:
        one.start()


def arrived(copies):
    for one in copies:
        one.wait_recv()


NT = (((1,), (1,)), ((), ()))
TN = (((0,), (0,)), ((), ()))
NN = (((1,), (0,)), ((), ()))


def dot(a, b, dims):
    return lax.dot_general(a, b, dims, preferred_element_type=jnp.float32)


def kernel(
    n_exp, n_ctx, cap,
    tok_in, cot_in, ids_row, weight_row, w_gate, w_up, w_down,
    token_out, route_out, gate_grad, up_grad, down_grad,
    tok, cot, scaled, scaled_far, ids_far, table, send_x, x_rows, send_y, y_rows,
    gate_w, up_w, down_w, gate_t, up_t, down_t,
    pre_send, pre_got, pre, slope, back_send, back_got, hid_all, d_all, x_two, y_two,
    back, home, inner, home_inner,
    keep, sum_send, sum_got, keep_down, down_send, down_got, tok_send, tok_got,
    send_sem, recv_sem, local_sem,
):
    me_exp = lax.axis_index("exp")
    me = lax.axis_index("ctx")
    bf, f32 = jnp.bfloat16, jnp.float32
    sib, across, along = ctx_neighbours(me)
    core = lax.rem(me, 2)
    side_x = lax.rem(lax.div(me, 2), 2)
    side_y = lax.div(me, 4)
    exp_peers = [lax.rem(me_exp + d, n_exp) for d in range(1, n_exp)]
    count, width = cot.shape
    cols = width // n_ctx
    rows = n_exp * cap
    wide, strip = width // 2, width // 4

    def cut(at, size):
        return pl.ds(pl.multiple_of(at * size, size), size)

    def part(base, size):
        return pl.ds(pl.multiple_of(base, 16), size)

    copies = Copies(send_sem, recv_sem, local_sem)
    remote, local = copies.remote, copies.local
    block, other = cut(side_y, wide), cut(1 - side_y, wide)
    loads = [local(cot_in, cot), local(tok_in.at[:, block], tok.at[0])]
    begin(loads)
    greeted = greet([sib, across, along], exp_peers)

    down_i = lax.broadcasted_iota(jnp.int32, (count, count), 0)
    over_i = lax.broadcasted_iota(jnp.int32, (count, count), 1)
    diagonal = down_i == over_i

    def fill_table(at, row):
        row_f = row.astype(f32)
        col_f = jnp.sum(jnp.where(diagonal, row_f, 0.0), axis=1, keepdims=True)
        position = jnp.sum(
            jnp.where((col_f == row_f) & (down_i < over_i), 1.0, 0.0), axis=0, keepdims=True
        )
        target = row * cap + position.astype(jnp.int32)
        places = lax.broadcasted_iota(jnp.int32, (rows, count), 0)
        table[at] = jnp.where(places == target, 1.0, 0.0).astype(bf)

    def place(at):
        return (lax.rem(at, 2) * 2 + lax.div(at, 2)) * cap

    def scatter(source, out, base):
        moves = [
            remote(
                source.at[part(base + peer * cap, cap)],
                out.at[part(base + place(me_exp), cap)],
                exp=peer,
            )
            for peer in exp_peers
        ]
        moves.append(
            local(
                source.at[part(base + me_exp * cap, cap)],
                out.at[part(base + place(me_exp), cap)],
            )
        )
        return moves

    def give_back(source, out, base, peers, own, at=slice(None)):
        moves = [
            remote(
                source.at[part(base + place(peer), cap), at],
                out.at[part(base + me_exp * cap, cap), at],
                exp=peer,
            )
            for peer in peers
        ]
        if own:
            moves.append(
                local(
                    source.at[part(base + place(me_exp), cap), at],
                    out.at[part(base + me_exp * cap, cap), at],
                )
            )
        begin(moves)
        return moves

    fill_table(0, ids_row[...])
    weight_col = jnp.sum(jnp.where(diagonal, weight_row[...], 0.0), axis=1, keepdims=True)
    loads[0].wait()
    scaled[...] = (weight_col * cot[...].astype(f32)).astype(bf)
    loads[1].wait()
    send_x[:rows] = dot(table[0], tok[0], NN).astype(bf)

    def gathered(own, out, at, at_peer, peer):
        return (
            remote(own.at[0], out.at[at], ctx=peer),
            remote(own.at[0], out.at[at], ctx=sib),
            remote(out.at[at_peer], out.at[at_peer], ctx=sib),
            local(own.at[0], out.at[at]),
        )

    at, at_across = cut(lax.rem(me, 4), cols), cut(lax.rem(across, 4), cols)
    side_w = [gathered(own, out, at, at_across, across) for own, out in ((w_gate, gate_w), (w_up, up_w))]
    side_w.append(gathered(w_down, down_w, side_y * 2 + core, (1 - side_y) * 2 + core, along))
    spread_x = [
        remote(ids_row, ids_far.at[0], ctx=along),
        remote(tok_in.at[:, other], tok.at[1], ctx=along),
    ]
    spread_y = [remote(ids_row, ids_far.at[1], ctx=across)] + [
        remote(
            scaled.at[:, cut(2 * s + 1 - side_x, strip)],
            scaled_far.at[:, s * strip:(s + 1) * strip],
            ctx=across,
        )
        for s in range(2)
    ]
    sent_x = [scatter(send_x, x_rows, base) for base in (0, rows)]
    sent_y = [scatter(send_y, y_rows, base) for base in (0, rows)]
    pl.semaphore_wait(pltpu.get_barrier_semaphore(), greeted)
    begin(spread_x)
    begin(spread_y)
    begin(sent_x[0])
    for g in side_w:
        g[0].start()
    for s in range(2):
        send_y[:rows, s * strip:(s + 1) * strip] = dot(
            table[0], scaled[:, cut(2 * s + side_x, strip)], NN
        ).astype(bf)
    spread_x[0].wait_recv()
    fill_table(1, ids_far[0])
    spread_x[1].wait_recv()
    send_x[rows:] = dot(table[1], tok[1], NN).astype(bf)
    begin(sent_x[1])
    for g in side_w:
        begin(g[1::2])
    spread_y[0].wait_recv()
    fill_table(2, ids_far[1])
    arrived(spread_y[1:])
    send_y[rows:] = dot(table[2], scaled_far[...], NN).astype(bf)

    def all_here(g):
        g[3].wait()
        g[1].wait_recv()
        g[2].wait_recv()

    def pass_on(g):
        g[0].wait_recv()
        g[2].start()

    pre_moves = [remote(pre_send.at[m], pre_got.at[m], ctx=along) for m in (0, 1)]
    pass_on(side_w[0])
    begin(sent_y[1])
    pass_on(side_w[2])
    arrived(sent_x[0])
    all_here(side_w[0])
    pre[0] = dot(x_rows[:rows], gate_w[...], NN)
    begin(sent_y[0])
    arrived(sent_x[1])
    pre_send[0] = dot(x_rows[rows:], gate_w[...], NN).astype(bf)
    pre_moves[0].start()
    pair = cut(core, 2 * rows)

    def pair_up(source, out):
        moves = []
        for q in range(2):
            moves.append(
                remote(source.at[:, cut(2 * q + 1 - core, cols)], out.at[q, pair], ctx=sib)
            )
            moves.append(local(source.at[:, cut(2 * q + core, cols)], out.at[q, pair]))
        begin(moves)
        return moves

    paired_x = pair_up(x_rows, x_two)
    all_here(side_w[2])
    for q in range(4):
        down_t[q * cols:(q + 1) * cols] = down_w[q].T
    pass_on(side_w[1])
    all_here(side_w[1])
    pre_send[1] = dot(x_rows[rows:], up_w[...], NN).astype(bf)
    pre_moves[1].start()
    pre[1] = dot(x_rows[:rows], up_w[...], NN)
    back_move = remote(back_send, back_got, ctx=across)
    arrived(sent_y[1])
    back_send[...] = dot(y_rows[rows:], down_t[...], NN).astype(bf)
    back_move.start()
    gate_t[...] = gate_w[...].T
    up_t[...] = up_w[...].T

    ours = part(core * 2 * rows, rows)
    theirs = part(core * 2 * rows + rows, rows)
    hid_across = remote(hid_all.at[ours], hid_all.at[theirs], ctx=across)
    hid_sib = [remote(hid_all.at[at], hid_all.at[at], ctx=sib) for at in (ours, theirs)]
    pre_moves[0].wait_recv()
    gate = pre[0] + pre_got[0].astype(f32)
    sig = 1.0 / (1.0 + jnp.exp(-gate))
    pre[0] = gate * sig
    slope[...] = sig * (1.0 + gate * (1.0 - sig))
    arrived(sent_y[0])
    paired_y = pair_up(y_rows, y_two)
    back_sum = dot(y_rows[:rows], down_t[...], NN)
    back_move.wait_recv()
    back_sum = back_sum + back_got[...].astype(f32)
    low = lax.rem(me_exp, 2)
    base = core * 2 * rows + rows
    halves = [part(base - rows + at * 2 * cap, 2 * cap) for at in (low, 1 - low)]
    far_halves = [part(base + at * 2 * cap, 2 * cap) for at in (low, 1 - low)]
    units = d_all.shape[2]
    pieces = [(1, pl.ds(0, units // 2)), (1, pl.ds(units // 2, units // 2)), (0, pl.ds(0, units))]
    first_along = [
        remote(d_all.at[1, ours, at], d_all.at[1, theirs, at], ctx=along) for _, at in pieces[:2]
    ]
    second_along = [
        remote(d_all.at[0, a], d_all.at[0, b], ctx=along) for a, b in zip(halves, far_halves)
    ]
    ours_sib = [remote(d_all.at[m, ours], d_all.at[m, ours], ctx=sib) for m in (0, 1)]
    theirs_sib = [
        remote(d_all.at[m, theirs, at], d_all.at[m, theirs, at], ctx=sib) for m, at in pieces
    ]
    d_all[1, ours] = (back_sum * pre[0]).astype(bf)
    begin(first_along)
    ours_sib[1].start()
    pre_moves[1].wait_recv()
    up = pre[1] + pre_got[1].astype(f32)
    d_all[0, ours] = (back_sum * up * slope[...]).astype(bf)
    begin(second_along)
    ours_sib[0].start()
    hid_all[ours] = (pre[0] * up).astype(bf)
    hid_across.start()
    hid_sib[0].start()

    def slot_rows(to, at):
        back[to] = (
            dot(d_all[0, at], gate_t[...], NN) + dot(d_all[1, at], up_t[...], NN)
        ).astype(bf)

    inner[...] = jnp.broadcast_to(
        jnp.sum(hid_all[ours].astype(f32) * back_sum, axis=1, keepdims=True), inner.shape
    )
    slot_rows(part(0, rows), ours)
    home_own = give_back(back, home, 0, exp_peers, True)
    home_own += give_back(inner, home_inner, 0, exp_peers, True)

    hid_across.wait_recv()
    hid_sib[1].start()
    arrived(paired_x)
    arrived(paired_y)
    sum_moves = [remote(sum_send.at[m, :, at], sum_got.at[m, :, at], ctx=across) for m, at in pieces]

    def side_sum(k):
        m, at = pieces[k]
        if k != 1:
            ours_sib[m].wait_recv()
        theirs_sib[k].wait_recv()
        sum_send[m, :, at] = dot(x_two[1 - side_x], d_all[m, :, at], TN).astype(bf)
        sum_moves[k].start()

    first_along[0].wait_recv()
    theirs_sib[0].start()
    side_sum(0)
    first_along[1].wait_recv()
    theirs_sib[1].start()
    arrived(hid_sib)
    down_move = remote(down_send, down_got, ctx=along)
    down_send[...] = dot(hid_all[...], y_two[1 - side_y], TN).astype(bf)
    down_move.start()
    side_sum(1)
    second_along[0].wait_recv()
    slot_rows(part(rows + low * 2 * cap, 2 * cap), far_halves[0])
    home_far = give_back(back, home, rows, exp_peers[1:2], True)
    second_along[1].wait_recv()
    theirs_sib[2].start()
    slot_rows(part(rows + (1 - low) * 2 * cap, 2 * cap), far_halves[1])
    strips = [pl.ds(q * cols, cols) for q in range(4)]
    home_last = [give_back(back, home, rows, exp_peers[::2], False, at) for at in strips]
    side_sum(2)
    keep_down[...] = dot(hid_all[...], y_two[side_y], TN)
    keep[1] = dot(x_two[side_x], d_all[1], TN)
    keep[0] = dot(x_two[side_x], d_all[0], TN)

    arrived(home_own)
    token_out[:, block] = dot(table[0], home[:rows], TN).astype(bf)
    route_out[...] = (
        jnp.sum(table[0].astype(f32) * home_inner[...], axis=0, keepdims=True) / weight_row[...]
    )
    arrived(home_far)
    tok_moves = [remote(tok_send.at[:, at], tok_got.at[:, at], ctx=along) for at in strips]
    for last, at, move in zip(home_last, strips, tok_moves):
        arrived(last)
        tok_send[:, at] = dot(table[1], home[rows:, at], TN).astype(bf)
        move.start()
    down_move.wait_recv()
    down_grad[...] = (keep_down[...] + down_got[...].astype(f32)).astype(bf)
    for m, out in ((1, up_grad), (0, gate_grad)):
        arrived(sum_moves[:2] if m else sum_moves[2:])
        out[...] = (keep[m] + sum_got[m].astype(f32)).astype(bf)
    arrived(tok_moves)
    token_out[:, other] = tok_got[...]
    copies.sent()


def hand_over(*refs):
    for source, out in zip(refs[:5], refs[5:]):
        out[...] = source[...]


def fast_body(tokens, cotangent, expert_ids, route_weights, w_gate, w_up, w_down):
    n_ctx = lax.axis_size("ctx")
    n_exp = lax.axis_size("exp")
    count, width = tokens.shape
    cap = max(2, (3 * count + 2 * n_exp - 1) // (2 * n_exp))
    cols = width // n_ctx
    units = w_gate.shape[2]
    rows = n_exp * cap
    wide = width // 2
    bf, f32 = jnp.bfloat16, jnp.float32
    vm = pl.BlockSpec(memory_space=pltpu.VMEM)
    hbm = pl.BlockSpec(memory_space=pl.ANY)
    dma = pltpu.SemaphoreType.DMA
    scratch = [
        ((2, count, wide), bf), ((count, width), bf), ((count, width), bf), ((count, wide), bf),
        ((2, 1, count), jnp.int32), ((3, rows, count), bf),
        ((2 * rows, wide), bf), ((2 * rows, wide), bf), ((2 * rows, wide), bf), ((2 * rows, wide), bf),
        ((wide, units), bf), ((wide, units), bf), ((n_ctx // 2, units, cols), bf),
        ((units, wide), bf), ((units, wide), bf), ((wide, units), bf),
        ((2, rows, units), bf), ((2, rows, units), bf), ((2, rows, units), f32),
        ((rows, units), f32),
        ((rows, units), bf), ((rows, units), bf),
        ((4 * rows, units), bf), ((2, 4 * rows, units), bf),
        ((2, 4 * rows, cols), bf), ((2, 4 * rows, cols), bf),
        ((2 * rows, wide), bf), ((2 * rows, wide), bf),
        ((rows, count), f32), ((rows, count), f32),
        ((2, cols, units), f32), ((2, cols, units), bf), ((2, cols, units), bf),
        ((units, cols), f32), ((units, cols), bf), ((units, cols), bf),
        ((count, wide), bf), ((count, wide), bf),
    ]
    token_grads, route, gate_grads, up_grads, down_grads = pl.pallas_call(
        functools.partial(kernel, n_exp, n_ctx, cap),
        out_shape=(
            jax.ShapeDtypeStruct((count, width), bf),
            jax.ShapeDtypeStruct((1, count), f32),
            jax.ShapeDtypeStruct((cols, units), bf),
            jax.ShapeDtypeStruct((cols, units), bf),
            jax.ShapeDtypeStruct((units, cols), bf),
        ),
        in_specs=[hbm] * 2 + [vm] * 2 + [hbm] * 3,
        out_specs=(vm,) * 5,
        scratch_shapes=[pltpu.VMEM(*one) for one in scratch] + [dma((80,)), dma((80,)), dma((40,))],
        compiler_params=pltpu.CompilerParams(
            collective_id=0, has_side_effects=True, vmem_limit_bytes=56 * 1024 * 1024
        ),
    )(
        tokens, cotangent, expert_ids.reshape(1, count), route_weights.reshape(1, count),
        w_gate, w_up, w_down,
    )
    results = (token_grads, route, gate_grads, up_grads, down_grads)
    token_grads, route, gate_grads, up_grads, down_grads = pl.pallas_call(
        hand_over,
        out_shape=tuple(jax.ShapeDtypeStruct(r.shape, r.dtype) for r in results),
        in_specs=[vm] * 5,
        out_specs=(vm,) * 5,
    )(*results)
    return (
        token_grads, route.reshape(count, 1), gate_grads[None], up_grads[None], down_grads[None]
    )


def solution(mesh):
    return jax.shard_map(
        fast_body if (mesh.shape["ctx"], mesh.shape["exp"]) == (8, 4) else body,
        mesh=mesh,
        in_specs=(
            P(("ctx", "exp"), None),
            P(("ctx", "exp"), None),
            P(("ctx", "exp"), None),
            P(("ctx", "exp"), None),
            P("exp", "ctx", None),
            P("exp", "ctx", None),
            P("exp", None, "ctx"),
        ),
        out_specs=(
            P(("ctx", "exp"), None),
            P(("ctx", "exp"), None),
            P("exp", "ctx", None),
            P("exp", "ctx", None),
            P("exp", None, "ctx"),
        ),
        check_vma=False,
    )
```
